128 devices in a mesh: row: 16 (over x, y), col: 8 (over z, core).
Axes of the slice: x: 4, y: 4, z: 4, core: 2. Of those that a mesh axis runs over, the one named last changes fastest.
Arguments:
- density: bfloat16 [16384, 16384], P('row', 'col'), as said below
- block_mask: int32 [128, 128], P('row', 'col'), may hold values from 0 to 1, as said below
Outputs:
- purified_slab: float32 [1024, 16384], P('col', 'row')
The draws below stay inside these ranges and needn't reach their ends.
Inputs may be any that keep to these rules, and one draw needn't show every extreme that they name: density is exactly symmetric. block_mask is symmetric and its diagonal is all ones.
All inputs are finite; a program needn't handle non-finite values.
Results may differ from the reference program's by a relative error of at most 0.0018.
Values may be sent and summed in bfloat16 or wider, within the bound.
No kernel may reach another device: no remote copies, remote signals or barrier semaphores. Data moves between devices by JAX's collectives and lax.ppermute only.
A program may use at most 128 MiB of HBM per device.

```python
import jax
import jax.numpy as jnp

BLOCK = 128
SLAB = 1024
NMAT = 16384
NBLK = 128


def draw_density(key, part):
    base = jax.random.normal(key, (NMAT, NMAT), jnp.float32)
    spread = (0.45 * NMAT) ** (-0.5)
    return ((base + base.T) * (0.70710678 * spread)).astype(jnp.bfloat16)


def draw_block_mask(key, part):
    row_rates = jax.random.randint(jax.random.fold_in(key, 1), (NBLK,), 2, 7)
    ticket = jax.random.randint(jax.random.fold_in(key, 2), (NBLK, NBLK), 0, 32)
    chosen = (ticket < row_rates[:, None] * row_rates[None, :]).astype(jnp.int32)
    position = jnp.arange(NBLK)
    upper_part = jnp.where(position[:, None] <= position[None, :], chosen, chosen.T)
    return jnp.maximum(upper_part, jnp.eye(NBLK, dtype=jnp.int32))


def setup_inputs(seed: int = 0) -> dict:
    streams_of = jax.random.split(jax.random.key(seed), 3)
    density = draw_density(jax.random.fold_in(streams_of[2], 71), 0)
    block_mask = draw_block_mask(jax.random.fold_in(streams_of[2], 71), 0)
    return {"density": density, "block_mask": block_mask}


def reference(density, block_mask):
    mask_full = jnp.repeat(jnp.repeat(block_mask.astype(jnp.bfloat16), BLOCK, 0), BLOCK, 1)
    masked = density * mask_full
    slab_rows = masked[:SLAB]
    square_full = jnp.dot(slab_rows, masked, preferred_element_type=jnp.float32)
    square_slab = square_full.astype(jnp.bfloat16)
    cube = jnp.dot(square_slab, masked, preferred_element_type=jnp.float32)
    return 3.0 * square_full - 2.0 * cube
```

```python
import functools

import jax
import jax.numpy as jnp
from jax import lax
from jax.experimental import pallas as pl
from jax.experimental.pallas import tpu as pltpu
from jax.sharding import Mesh
from jax.sharding import PartitionSpec as P

BLOCK = 128
SLAB = 1024
WIDE = 2048
LANES = 128
QUARTER = SLAB // 4
PIECE = SLAB // 16
LINE = ("x", "y", "core")
F32, BF16, I16, I32 = jnp.float32, jnp.bfloat16, jnp.int16, jnp.int32

FIRST, SECOND, DEPTH, CORE, OWNER, HALF = range(6)


def shape(rows, columns, dtype):
    return jax.ShapeDtypeStruct((rows, columns), dtype)


def encode(v):
    top = jnp.max(jnp.abs(v), axis=1, keepdims=True)
    e = jnp.clip(jnp.floor(jnp.log2(top)) + 1.0, -100.0, 128.0)
    q = jnp.clip(jnp.round(v * jnp.exp2(15.0 - e)), -32767.0, 32767.0)
    tail = jnp.broadcast_to(e, (v.shape[0], LANES))
    return q.astype(I32).astype(I16), tail.astype(I32).astype(I16)


def put(ref, v):
    q, tail = encode(v)
    width = v.shape[1]
    ref[:, :width] = q
    ref[:, width:] = tail


def take(ref):
    width = ref.shape[1] - LANES
    e = ref[:, width:].astype(I32).astype(F32)
    scale = jnp.exp2(e - 15.0)[:, :1]
    return ref[:, :width].astype(I32).astype(F32) * scale


def first_kernel(d, s, own, other, top, low, out, acc):
    n = pl.program_id(0)
    dims = (((0,), (0,)), ((), ()))
    t = lax.dot_general(own[...], top[...], dims, preferred_element_type=F32)
    t += lax.dot_general(other[...], low[...], dims, preferred_element_type=F32)
    if d == 0:
        out[...] = t
    else:
        acc[:, pl.ds(pl.multiple_of(n * 512, 512), 512)] = t

        @pl.when(n == pl.num_programs(0) - 1)
        def _():
            put(out, acc[...])


def first_product(d, s, own, other, masked):
    if d == 0:
        out = shape(QUARTER, WIDE, F32)
        out_spec = pl.BlockSpec((QUARTER, 512), lambda n, s: (0, n))
    else:
        out = shape(QUARTER, WIDE + LANES, I16)
        out_spec = pl.BlockSpec((QUARTER, WIDE + LANES), lambda n, s: (0, 0))
    piece = pl.BlockSpec((512, QUARTER), lambda n, s: (0, (s[FIRST] + d) % 4))
    return pl.pallas_call(
        functools.partial(first_kernel, d),
        out_shape=out,
        grid_spec=pltpu.PrefetchScalarGridSpec(
            num_scalar_prefetch=1,
            grid=(WIDE // 512,),
            in_specs=[
                piece,
                piece,
                pl.BlockSpec((512, 512), lambda n, s: (s[CORE], n)),
                pl.BlockSpec((512, 512), lambda n, s: (1 - s[CORE], n)),
            ],
            out_specs=out_spec,
            scratch_shapes=[pltpu.VMEM((QUARTER, WIDE), F32)],
        ),
        cost_estimate=pl.CostEstimate(
            flops=2 * QUARTER * SLAB * WIDE, bytes_accessed=6 << 20, transcendentals=0
        ),
        name=f"first_{d}",
    )(s, own, other, masked, masked)


def spread_kernel(s, own, a, b, c, out0, out1, out2, out3):
    g = pl.program_id(0)
    v = own[...] + take(a) + take(b) + take(c)

    @pl.when(g == 0)
    def _():
        out0[...] = v

    for d, out in enumerate((out1, out2, out3), 1):

        @pl.when(g == d)
        def _(out=out):
            put(out, v)


def spread_sum(s, own, parts):
    index = lambda g, s: ((s[SECOND] + g) % 4, 0)
    fixed = lambda g, s: (0, 0)
    coded = WIDE + LANES
    return pl.pallas_call(
        spread_kernel,
        out_shape=[shape(PIECE, WIDE, F32)] + [shape(PIECE, coded, I16)] * 3,
        grid_spec=pltpu.PrefetchScalarGridSpec(
            num_scalar_prefetch=1,
            grid=(4,),
            in_specs=[pl.BlockSpec((PIECE, WIDE), index)]
            + [pl.BlockSpec((PIECE, coded), index)] * 3,
            out_specs=[pl.BlockSpec((PIECE, WIDE), fixed)]
            + [pl.BlockSpec((PIECE, coded), fixed)] * 3,
        ),
        cost_estimate=pl.CostEstimate(
            flops=8 << 20, bytes_accessed=6 << 20, transcendentals=0
        ),
        name="spread",
    )(s, own, *parts)


def gather_kernel(own, a, b, c, out):
    put(out, own[...] + take(a) + take(b) + take(c))


def finish_kernel(own, a, b, c, out):
    out[...] = own[...] + take(a) + take(b) + take(c)


def second_kernel(first, s, coded, block, *refs):
    mine, theirs, rounded, triple = refs if first else refs[2:]
    n = pl.program_id(0)

    @pl.when(n == 0)
    def _():
        for j in range(4):
            sub = (s[SECOND] + 4 - j) % 4
            place = ((sub // 2) ^ s[CORE]) * 128 + (sub % 2) * 64
            rows = pl.ds(pl.multiple_of(place, 64), PIECE)
            v = take(coded.at[j * PIECE : (j + 1) * PIECE])
            rounded[rows, :] = v.astype(BF16)
            for half in range(2):

                @pl.when((s[OWNER] == 1) & (s[HALF] == half))
                def _(v=v, rows=rows, half=half):
                    triple[rows, :] = 3.0 * v[:, half * SLAB : (half + 1) * SLAB]

    t = -2.0 * lax.dot_general(
        rounded[...], block[...], (((1,), (1,)), ((), ())), preferred_element_type=F32
    )

    @pl.when(s[OWNER] == 1)
    def _():
        u = t + triple[:, pl.ds(pl.multiple_of(n * 256, 256), 256)]
        mine[...] = u[:128]
        theirs[...] = u[128:]

    @pl.when(s[OWNER] == 0)
    def _():
        mine[...] = t[:128]
        theirs[...] = t[128:]


def second_product(d, s, coded, masked, kept):
    first = kept is None
    whole = pl.BlockSpec((128, 256), lambda n, s: ((s[FIRST] + 4 - d) % 4, n))
    extra = [] if first else [pl.BlockSpec(memory_space=pl.ANY)] * 2
    return pl.pallas_call(
        functools.partial(second_kernel, first),
        out_shape=[shape(512, SLAB, F32)] * 2,
        grid_spec=pltpu.PrefetchScalarGridSpec(
            num_scalar_prefetch=1,
            grid=(4,),
            in_specs=[
                pl.BlockSpec((QUARTER, WIDE + LANES), lambda n, s: (0, 0)),
                pl.BlockSpec((256, WIDE), lambda n, s: (n, 0)),
            ]
            + extra,
            out_specs=[whole, whole],
            scratch_shapes=[
                pltpu.VMEM((QUARTER, WIDE), BF16),
                pltpu.VMEM((QUARTER, SLAB), F32),
            ],
        ),
        input_output_aliases={} if first else {3: 0, 4: 1},
        cost_estimate=pl.CostEstimate(
            flops=2 * QUARTER * SLAB * WIDE, bytes_accessed=6 << 20, transcendentals=0
        ),
        name=f"second_{d}",
    )(s, coded, masked, *(() if first else kept))


def deal_kernel(s, mine, came, out0, out1, out2, out3):
    g = pl.program_id(0)
    v = mine[...] + came[...]

    @pl.when(g == 0)
    def _():
        out0[...] = v

    for d, out in enumerate((out1, out2, out3), 1):

        @pl.when(g == d)
        def _(out=out):
            put(out, v)


def deal(s, mine, came):
    index = lambda g, s: ((s[DEPTH] + g) % 4, 0)
    fixed = lambda g, s: (0, 0)
    return pl.pallas_call(
        deal_kernel,
        out_shape=[shape(128, SLAB, F32)] + [shape(128, SLAB + LANES, I16)] * 3,
        grid_spec=pltpu.PrefetchScalarGridSpec(
            num_scalar_prefetch=1,
            grid=(4,),
            in_specs=[pl.BlockSpec((128, SLAB), index)] * 2,
            out_specs=[pl.BlockSpec((128, SLAB), fixed)]
            + [pl.BlockSpec((128, SLAB + LANES), fixed)] * 3,
        ),
        cost_estimate=pl.CostEstimate(
            flops=4 << 20, bytes_accessed=5 << 20, transcendentals=0
        ),
        name="deal",
    )(s, mine, came)


def place(x, y, core):
    return (x * 4 + y) * 2 + core


def along(v, d, first):
    pairs = []
    for x in range(4):
        for y in range(4):
            for core in range(2):
                to = ((x + d) % 4, y) if (core == 0) == first else (x, (y + d) % 4)
                pairs.append((place(x, y, core), place(*to, core)))
    return lax.ppermute(v, LINE, pairs)


def swap(v):
    return lax.ppermute(v, "core", [(0, 1), (1, 0)])


def spread_column(piece, z, core):
    rows = piece.shape[0] // 2
    came = lax.ppermute(piece[rows:], "core", [(0, 1), (1, 0)])
    half = jnp.where(core == 0, piece[:rows], came)
    axes = ("z", "core")
    came = lax.ppermute(half, axes, [(0, 2), (1, 7)])
    half = jnp.where(z == 0, half, came)
    came = lax.ppermute(half, axes, [(0, 6), (1, 3), (2, 4), (7, 5)])
    late = (z == 2) | ((z == 3) & (core == 0)) | ((z == 1) & (core == 1))
    return jnp.where(late, came, half)


def local(density, block_mask):
    x, y, z, core = (lax.axis_index(a) for a in ("x", "y", "z", "core"))
    row = x * 4 + y
    first = jnp.where(core == 0, x, y)
    second = jnp.where(core == 0, y, x)
    owner = (z * 2 + core == row // 2).astype(I32)
    s = jnp.zeros((8,), I32)
    at = jnp.arange(8, dtype=I32)
    for i, v in enumerate((first, second, z, core, owner, row % 2)):
        s = jnp.where(at == i, v, s)

    wide = jnp.repeat(block_mask.astype(BF16), BLOCK, 1)
    masked = (density.reshape(8, BLOCK, WIDE) * wide[:, None, :]).reshape(SLAB, WIDE)
    own = spread_column(masked[:, :SLAB], z, core)
    other = swap(own)

    came = [along(first_product(d, s, own, other, masked), d, True) for d in (2, 1, 3)]
    mine = first_product(0, s, own, other, masked)
    mine, *parts = spread_sum(s, mine, came)
    came = [along(v, d, False) for d, v in ((2, parts[1]), (1, parts[0]), (3, parts[2]))]
    coded = pl.pallas_call(
        gather_kernel, out_shape=shape(PIECE, WIDE + LANES, I16), name="gather"
    )(mine, *came)

    near = [along(coded, d, False) for d in (1, 2, 3)]
    coded = jnp.concatenate([coded, *near], 0)
    far = {d: along(coded, d, True) for d in (1, 2, 3)}
    kept = second_product(0, s, coded, masked, None)
    for d in (1, 3, 2):
        kept = second_product(d, s, far[d], masked, kept)
    mine, *parts = deal(s, kept[0], swap(kept[1]))
    came = [
        lax.ppermute(parts[d - 1], "z", [(i, (i + d) % 4) for i in range(4)])
        for d in (2, 1, 3)
    ]
    return pl.pallas_call(finish_kernel, out_shape=shape(128, SLAB, F32), name="finish")(
        mine, *came
    )


def solution(mesh):
    torus = Mesh(mesh.devices.reshape(4, 4, 4, 2), ("x", "y", "z", "core"))
    in_specs = (P(("x", "y"), ("z", "core")),) * 2
    out_specs = P(("z", "core"), ("x", "y"))
    return jax.shard_map(local, mesh=torus, in_specs=in_specs, out_specs=out_specs, check_vma=False)
```

```python
import functools

import jax
import jax.numpy as jnp
from jax import lax
from jax.experimental import pallas as pl
from jax.experimental.pallas import tpu as pltpu
from jax.sharding import Mesh
from jax.sharding import PartitionSpec as P

BLOCK = 128
SLAB = 1024
WIDE = 2048
LANES = 128
QUARTER = SLAB // 4
PIECE = SLAB // 16
AXES = ("x", "y", "z", "core")
F32, BF16, I16, I32 = jnp.float32, jnp.bfloat16, jnp.int16, jnp.int32

SENT = ((1, 0, 0, 0), (2, 2, 1, 1), (3, 3, 3, 2))
SECOND, CORE, OWNER, HALF, BASE = range(4, 9)


def shape(rows, columns, dtype):
    return jax.ShapeDtypeStruct((rows, columns), dtype)


def call(kernel, out, s, *args, name, flops=1 << 22, scratch=()):
    in_vmem = pl.BlockSpec(memory_space=pltpu.VMEM)
    return pl.pallas_call(
        kernel,
        out_shape=out,
        in_specs=[pl.BlockSpec(memory_space=pltpu.SMEM)] * len(s) + [in_vmem] * len(args),
        out_specs=jax.tree.map(lambda _: in_vmem, out),
        scratch_shapes=list(scratch),
        compiler_params=pltpu.CompilerParams(vmem_limit_bytes=16 << 20),
        cost_estimate=pl.CostEstimate(flops=flops, bytes_accessed=4 << 20, transcendentals=0),
        name=name,
    )(*s, *args)


def encode(v):
    top = jnp.max(jnp.abs(v), axis=1, keepdims=True)
    e = jnp.clip(jnp.floor(jnp.log2(top)) + 1.0, -100.0, 128.0)
    q = jnp.clip(jnp.round(v * jnp.exp2(15.0 - e)), -32767.0, 32767.0)
    tail = jnp.broadcast_to(e, (v.shape[0], LANES))
    return q.astype(I32).astype(I16), tail.astype(I32).astype(I16)


def put(ref, v):
    q, tail = encode(v)
    width = v.shape[1]
    ref[:, :width] = q
    ref[:, width:] = tail


def take(ref, rows=slice(None)):
    width = ref.shape[1] - LANES
    e = ref[rows, width:].astype(I32).astype(F32)
    scale = jnp.exp2(e - 15.0)[:, :1]
    return ref[rows, :width].astype(I32).astype(F32) * scale


def at(i, size):
    return pl.ds(pl.multiple_of(i * size, size), size)


def masked_block(m, density, i, j):
    block = density[i * BLOCK : (i + 1) * BLOCK, j * BLOCK : (j + 1) * BLOCK]
    return jnp.where(m[i, j] != 0, block, jnp.zeros_like(block))


def column_kernel(s, m, density, top_a, low_a, top_b, low_b, whole):
    for i in range(8):
        for j in range(8):
            whole[i * BLOCK : (i + 1) * BLOCK, j * BLOCK : (j + 1) * BLOCK] = masked_block(m, density, i, j)
    for i, (top, low) in enumerate(((top_a, low_a), (top_b, low_b))):
        for j in range(2):
            columns = at((s[BASE] + 2 * i + j) % 4, QUARTER)
            to = slice(j * QUARTER, (j + 1) * QUARTER)
            top[:, to] = whole[:512, columns]
            low[:, to] = whole[512:, columns]


def mask_kernel(m, density, out):
    for i in range(8):
        for j in range(16):
            out[i * BLOCK : (i + 1) * BLOCK, j * BLOCK : (j + 1) * BLOCK] = masked_block(m, density, i, j)


def first_kernel(i, coded, s, *refs):
    *parts, masked, out, left, acc = refs
    for half, (own, other) in enumerate(zip(parts[::2], parts[1::2])):

        @pl.when(s[i] // 2 == half)
        def _(own=own, other=other):
            left[:512] = own[:, at(s[i] % 2, QUARTER)]
            left[512:] = other[:, at(s[i] % 2, QUARTER)]

    dims = (((0,), (0,)), ((), ()))
    to = acc if coded else out
    for n in range(4):
        columns = slice(n * 512, (n + 1) * 512)
        to[:, columns] = lax.dot_general(
            left[:512], masked[at(s[CORE], 512), columns], dims, preferred_element_type=F32
        ) + lax.dot_general(
            left[512:], masked[at(1 - s[CORE], 512), columns], dims, preferred_element_type=F32
        )
    if coded:
        put(out, acc[...])


def first_product(i, s, parts, masked, coded=True):
    out = shape(QUARTER, WIDE + LANES, I16) if coded else shape(QUARTER, WIDE, F32)
    return call(
        functools.partial(first_kernel, i, coded),
        out,
        [s],
        *parts,
        masked,
        name=f"first_{i}",
        flops=2 * QUARTER * SLAB * WIDE,
        scratch=[pltpu.VMEM((SLAB, QUARTER), BF16), pltpu.VMEM((QUARTER, WIDE), F32)],
    )


def spread_kernel(s, own, a, b, c, *outs):
    for d, out in enumerate(outs):
        rows = at((s[SECOND] + d) % 4, PIECE)
        v = own[rows, :] + take(a, rows) + take(b, rows) + take(c, rows)
        if d == 0:
            out[...] = v
        else:
            put(out, v)


def gather_kernel(own, a, b, c, out):
    put(out, own[...] + take(a) + take(b) + take(c))


def join_kernel(*refs):
    *parts, out = refs
    for i, part in enumerate(parts):
        out[i * PIECE : (i + 1) * PIECE] = part[...]


def second_kernel(s, coded, masked, mine, theirs, left):
    pieces = []
    for j in range(4):
        sub = (s[SECOND] + 4 - j) % 4
        start = ((sub // 2) ^ s[CORE]) * 128 + (sub % 2) * 64
        rows = pl.ds(pl.multiple_of(start, 64), PIECE)
        left[rows, :] = take(coded, slice(j * PIECE, (j + 1) * PIECE)).astype(BF16)
        pieces.append((j, start))
    for n in range(4):
        columns = slice(n * 256, (n + 1) * 256)
        t = -2.0 * lax.dot_general(
            left[...],
            masked[columns, :],
            (((1,), (1,)), ((), ())),
            preferred_element_type=F32,
        )
        mine[:, columns] = t[:128]
        theirs[:, columns] = t[128:]

    for half in range(2):

        @pl.when((s[OWNER] == 1) & (s[HALF] == half))
        def _(half=half):
            for j, start in pieces:
                v = take(coded, slice(j * PIECE, (j + 1) * PIECE))
                v = 3.0 * v[:, half * SLAB : (half + 1) * SLAB]

                @pl.when(start < 128)
                def _(v=v, start=start):
                    mine[pl.ds(pl.multiple_of(start, 64), PIECE), :] += v

                @pl.when(start >= 128)
                def _(v=v, start=start):
                    theirs[pl.ds(pl.multiple_of(start - 128, 64), PIECE), :] += v


def second_product(j, s, coded, masked):
    return call(
        second_kernel,
        [shape(128, SLAB, F32)] * 2,
        [s],
        coded,
        masked,
        name=f"second_{j}",
        flops=2 * QUARTER * SLAB * WIDE,
        scratch=[pltpu.VMEM((QUARTER, WIDE), BF16)],
    )


def pair_kernel(mine, came, out):
    put(out, mine[...] + came[...])


def finish_kernel(a, b, c, d, out):
    out[...] = take(a) + take(b) + take(c) + take(d)


def place(x, y, z, core):
    return ((x % 4 * 4 + y % 4) * 4 + z % 4) * 2 + core


DEVICES = [(x, y, z, c) for x in range(4) for y in range(4) for z in range(4) for c in range(2)]


def send(v, to):
    return lax.ppermute(v, AXES, [(place(*d), place(*to(*d))) for d in DEVICES])


def own_quarter(y, x, z, core):
    return (z - jnp.where(core == 0, y, x)) & 3


def along(v, shift):
    def to(x, y, z, core):
        d = shift(x if core else y, z)
        return (x, y + d, z, core) if core else (x + d, y, z, core)

    return send(v, to)


def across(v, d):
    return send(v, lambda x, y, z, core: (x + d, y, z, core) if core else (x, y + d, z, core))


def swap(v):
    return lax.ppermute(v, "core", [(0, 1), (1, 0)])


def spread_column(top, low, z, core):
    came = lax.ppermute(low, "core", [(0, 1), (1, 0)])
    half = jnp.where(core == 0, top, came)
    axes = ("z", "core")
    came = lax.ppermute(half, axes, [(0, 2), (1, 7)])
    half = jnp.where(z == 0, half, came)
    came = lax.ppermute(half, axes, [(0, 6), (1, 3), (2, 4), (7, 5)])
    late = (z == 2) | ((z == 3) & (core == 0)) | ((z == 1) & (core == 1))
    half = jnp.where(late, came, half)
    return half, swap(half)


def coordinates():
    x, y, z, core = (lax.axis_index(a) for a in AXES)
    row = x * 4 + y
    own = own_quarter(y, x, z, core)
    values = [sum((own == i).astype(I32) * b for i, b in enumerate(sent)) for sent in SENT]
    values += [own, jnp.where(core == 0, y, x), core]
    values += [(z * 2 + core == row >> 1).astype(I32), row & 1, (x + y) & 3]
    s = jnp.zeros((16,), I32)
    index = jnp.arange(16, dtype=I32)
    for i, v in enumerate(values):
        s = jnp.where(index == i, v, s)
    return s, z, core


def local(density, block_mask):
    s, z, core = coordinates()
    top_a, low_a, top_b, low_b = call(
        column_kernel,
        [shape(512, 512, BF16)] * 4,
        [s, block_mask],
        density,
        name="column",
        scratch=[pltpu.VMEM((SLAB, SLAB), BF16)],
    )
    masked = call(mask_kernel, shape(SLAB, WIDE, BF16), [block_mask], density, name="mask")
    near = spread_column(top_a, low_a, z, core)
    far = spread_column(top_b, low_b, z, core)

    came = []
    for i, parts in enumerate((near, near + far, near + far)):
        v = first_product(i, s, parts, masked)
        came.append(along(v, lambda second, z: SENT[i][(z - second) % 4] - (z - second)))
    mine = first_product(3, s, near + far, masked, False)
    wide, coded = shape(PIECE, WIDE, F32), shape(PIECE, WIDE + LANES, I16)
    mine, *parts = call(spread_kernel, [wide, coded, coded, coded], [s], mine, *came, name="spread")
    came = [across(parts[d - 1], d) for d in (2, 1, 3)]
    v = call(gather_kernel, coded, [], mine, *came, name="gather")

    parts = [across(v, d) for d in (1, 2, 3)]
    v = call(join_kernel, shape(QUARTER, WIDE + LANES, I16), [], v, *parts, name="join")
    quarters = [along(v, lambda second, z: j - second) for j in range(4)]
    came = []
    for j, v in enumerate(quarters):
        mine, theirs = second_product(j, s, v, masked)
        v = call(pair_kernel, shape(128, SLAB + LANES, I16), [], mine, swap(theirs), name="pair")
        came.append(send(v, lambda x, y, z, core: (x, y, x + y + z - j, core)))
    return call(finish_kernel, shape(128, SLAB, F32), [], *came, name="finish")


def solution(mesh):
    torus = Mesh(mesh.devices.reshape(4, 4, 4, 2), AXES)
    in_specs = (P(("x", "y"), ("z", "core")),) * 2
    out_specs = P(("z", "core"), ("x", "y"))
    return jax.shard_map(local, mesh=torus, in_specs=in_specs, out_specs=out_specs, check_vma=False)
```

```python
import functools

import jax
import jax.numpy as jnp
from jax import lax
from jax.experimental import pallas as pl
from jax.experimental.pallas import tpu as pltpu
from jax.sharding import Mesh
from jax.sharding import PartitionSpec as P

BLOCK = 128
SLAB = 1024
WIDE = 2048
LANES = 128
QUARTER = SLAB // 4
PIECE = SLAB // 16
AXES = ("x", "y", "z", "core")
F32, BF16, I16, I32 = jnp.float32, jnp.bfloat16, jnp.int16, jnp.int32

SENT = ((1, 0, 0, 0), (2, 2, 1, 1), (3, 3, 3, 2))
SECOND, CORE, OWNER, HALF, BASE = range(4, 9)


def shape(rows, columns, dtype):
    return jax.ShapeDtypeStruct((rows, columns), dtype)


def call(kernel, out, s, *args, flops=1 << 22, scratch=()):
    in_vmem = pl.BlockSpec(memory_space=pltpu.VMEM)
    return pl.pallas_call(
        kernel,
        out_shape=out,
        in_specs=[pl.BlockSpec(memory_space=pltpu.SMEM)] * len(s) + [in_vmem] * len(args),
        out_specs=jax.tree.map(lambda _: in_vmem, out),
        scratch_shapes=list(scratch),
        compiler_params=pltpu.CompilerParams(vmem_limit_bytes=16 << 20),
        cost_estimate=pl.CostEstimate(flops=flops, bytes_accessed=4 << 20, transcendentals=0),
    )(*s, *args)


def encode(v):
    top = jnp.max(jnp.abs(v), axis=1, keepdims=True)
    e = jnp.clip(jnp.floor(jnp.log2(top)) + 1.0, -100.0, 128.0)
    q = jnp.clip(jnp.round(v * jnp.exp2(15.0 - e)), -32767.0, 32767.0)
    tail = jnp.broadcast_to(e, (v.shape[0], LANES))
    return q.astype(I32).astype(I16), tail.astype(I32).astype(I16)


def put(ref, v):
    q, tail = encode(v)
    width = v.shape[1]
    ref[:, :width] = q
    ref[:, width:] = tail


def take(ref, rows=slice(None)):
    width = ref.shape[1] - LANES
    e = ref[rows, width:].astype(I32).astype(F32)
    scale = jnp.exp2(e - 15.0)[:, :1]
    return ref[rows, :width].astype(I32).astype(F32) * scale


def at(i, size):
    return pl.ds(pl.multiple_of(i * size, size), size)


def masked_block(m, density, i, j):
    block = density[i * BLOCK : (i + 1) * BLOCK, j * BLOCK : (j + 1) * BLOCK]
    return jnp.where(m[i, j] != 0, block, jnp.zeros_like(block))


def column_kernel(s, m, density, top_a, low_a, top_b, low_b, whole):
    for i in range(8):
        for j in range(8):
            whole[i * BLOCK : (i + 1) * BLOCK, j * BLOCK : (j + 1) * BLOCK] = masked_block(m, density, i, j)
    for i, (top, low) in enumerate(((top_a, low_a), (top_b, low_b))):
        for j in range(2):
            columns = at((s[BASE] + 2 * i + j) % 4, QUARTER)
            to = slice(j * QUARTER, (j + 1) * QUARTER)
            top[:, to] = whole[:512, columns]
            low[:, to] = whole[512:, columns]


def mask_kernel(m, density, out):
    for i in range(8):
        for j in range(16):
            out[i * BLOCK : (i + 1) * BLOCK, j * BLOCK : (j + 1) * BLOCK] = masked_block(m, density, i, j)


def first_kernel(i, coded, s, *refs):
    *parts, masked, out, left, acc = refs
    for half, (own, other) in enumerate(zip(parts[::2], parts[1::2])):

        @pl.when(s[i] // 2 == half)
        def _(own=own, other=other):
            left[:512] = own[:, at(s[i] % 2, QUARTER)]
            left[512:] = other[:, at(s[i] % 2, QUARTER)]

    dims = (((0,), (0,)), ((), ()))
    to = acc if coded else out
    for n in range(4):
        columns = slice(n * 512, (n + 1) * 512)
        to[:, columns] = lax.dot_general(
            left[:512], masked[at(s[CORE], 512), columns], dims, preferred_element_type=F32
        ) + lax.dot_general(
            left[512:], masked[at(1 - s[CORE], 512), columns], dims, preferred_element_type=F32
        )
    if coded:
        put(out, acc[...])


def first_product(i, s, parts, masked, coded=True):
    out = shape(QUARTER, WIDE + LANES, I16) if coded else shape(QUARTER, WIDE, F32)
    return call(
        functools.partial(first_kernel, i, coded),
        out,
        [s],
        *parts,
        masked,
        flops=2 * QUARTER * SLAB * WIDE,
        scratch=[pltpu.VMEM((SLAB, QUARTER), BF16), pltpu.VMEM((QUARTER, WIDE), F32)],
    )


def spread_kernel(s, own, a, b, c, *outs):
    for d, out in enumerate(outs):
        rows = at((s[SECOND] + d) % 4, PIECE)
        v = own[rows, :] + take(a, rows) + take(b, rows) + take(c, rows)
        if d == 0:
            out[...] = v
        else:
            put(out, v)


def gather_kernel(own, a, b, c, out):
    put(out, own[...] + take(a) + take(b) + take(c))


def join_kernel(*refs):
    *parts, out = refs
    for i, part in enumerate(parts):
        out[i * PIECE : (i + 1) * PIECE] = part[...]


def second_kernel(s, coded, masked, mine, theirs, left):
    pieces = []
    for j in range(4):
        sub = (s[SECOND] + 4 - j) % 4
        start = ((sub // 2) ^ s[CORE]) * 128 + (sub % 2) * 64
        rows = pl.ds(pl.multiple_of(start, 64), PIECE)
        left[rows, :] = take(coded, slice(j * PIECE, (j + 1) * PIECE)).astype(BF16)
        pieces.append((j, start))
    for n in range(4):
        columns = slice(n * 256, (n + 1) * 256)
        t = -2.0 * lax.dot_general(
            left[...],
            masked[columns, :],
            (((1,), (1,)), ((), ())),
            preferred_element_type=F32,
        )
        mine[:, columns] = t[:128]
        theirs[:, columns] = t[128:]

    for half in range(2):

        @pl.when((s[OWNER] == 1) & (s[HALF] == half))
        def _(half=half):
            for j, start in pieces:
                v = take(coded, slice(j * PIECE, (j + 1) * PIECE))
                v = 3.0 * v[:, half * SLAB : (half + 1) * SLAB]

                @pl.when(start < 128)
                def _(v=v, start=start):
                    mine[pl.ds(pl.multiple_of(start, 64), PIECE), :] += v

                @pl.when(start >= 128)
                def _(v=v, start=start):
                    theirs[pl.ds(pl.multiple_of(start - 128, 64), PIECE), :] += v


def second_product(s, coded, masked):
    return call(
        second_kernel,
        [shape(128, SLAB, F32)] * 2,
        [s],
        coded,
        masked,
        flops=2 * QUARTER * SLAB * WIDE,
        scratch=[pltpu.VMEM((QUARTER, WIDE), BF16)],
    )


def pair_kernel(mine, came, out):
    put(out, mine[...] + came[...])


def finish_kernel(a, b, c, d, out):
    out[...] = take(a) + take(b) + take(c) + take(d)


def place(x, y, z, core):
    return ((x % 4 * 4 + y % 4) * 4 + z % 4) * 2 + core


DEVICES = [(x, y, z, c) for x in range(4) for y in range(4) for z in range(4) for c in range(2)]


def send(v, to):
    return lax.ppermute(v, AXES, [(place(*d), place(*to(*d))) for d in DEVICES])


def own_quarter(y, x, z, core):
    return (z - jnp.where(core == 0, y, x)) & 3


def along(v, shift):
    def to(x, y, z, core):
        d = shift(x if core else y, z)
        return (x, y + d, z, core) if core else (x + d, y, z, core)

    return send(v, to)


def across(v, d):
    return send(v, lambda x, y, z, core: (x + d, y, z, core) if core else (x, y + d, z, core))


def swap(v):
    return lax.ppermute(v, "core", [(0, 1), (1, 0)])


def spread_column(top, low, z, core):
    came = lax.ppermute(low, "core", [(0, 1), (1, 0)])
    half = jnp.where(core == 0, top, came)
    axes = ("z", "core")
    came = lax.ppermute(half, axes, [(0, 2), (1, 7)])
    half = jnp.where(z == 0, half, came)
    came = lax.ppermute(half, axes, [(0, 6), (1, 3), (2, 4), (7, 5)])
    late = (z == 2) | ((z == 3) & (core == 0)) | ((z == 1) & (core == 1))
    half = jnp.where(late, came, half)
    return half, swap(half)


def coordinates():
    x, y, z, core = (lax.axis_index(a) for a in AXES)
    row = x * 4 + y
    own = own_quarter(y, x, z, core)
    values = [sum((own == i).astype(I32) * b for i, b in enumerate(sent)) for sent in SENT]
    values += [own, jnp.where(core == 0, y, x), core]
    values += [(z * 2 + core == row >> 1).astype(I32), row & 1, (x + y) & 3]
    s = jnp.zeros((16,), I32)
    index = jnp.arange(16, dtype=I32)
    for i, v in enumerate(values):
        s = jnp.where(index == i, v, s)
    return s, z, core


def local(density, block_mask):
    s, z, core = coordinates()
    top_a, low_a, top_b, low_b = call(
        column_kernel,
        [shape(512, 512, BF16)] * 4,
        [s, block_mask],
        density,
        scratch=[pltpu.VMEM((SLAB, SLAB), BF16)],
    )
    masked = call(mask_kernel, shape(SLAB, WIDE, BF16), [block_mask], density)
    near = spread_column(top_a, low_a, z, core)
    far = spread_column(top_b, low_b, z, core)

    came = []
    for i, parts in enumerate((near, near + far, near + far)):
        v = first_product(i, s, parts, masked)
        came.append(along(v, lambda second, z: SENT[i][(z - second) % 4] - (z - second)))
    mine = first_product(3, s, near + far, masked, False)
    wide, coded = shape(PIECE, WIDE, F32), shape(PIECE, WIDE + LANES, I16)
    mine, *parts = call(spread_kernel, [wide, coded, coded, coded], [s], mine, *came)
    came = [across(parts[d - 1], d) for d in (2, 1, 3)]
    v = call(gather_kernel, coded, [], mine, *came)

    parts = [across(v, d) for d in (1, 2, 3)]
    v = call(join_kernel, shape(QUARTER, WIDE + LANES, I16), [], v, *parts)
    quarters = [along(v, lambda second, z: j - second) for j in range(4)]
    came = []
    for j, v in enumerate(quarters):
        mine, theirs = second_product(s, v, masked)
        v = call(pair_kernel, shape(128, SLAB + LANES, I16), [], mine, swap(theirs))
        came.append(send(v, lambda x, y, z, core: (x, y, x + y + z - j, core)))
    return call(finish_kernel, shape(128, SLAB, F32), [], *came)


def solution(mesh):
    torus = Mesh(mesh.devices.reshape(4, 4, 4, 2), AXES)
    in_specs = (P(("x", "y"), ("z", "core")),) * 2
    out_specs = P(("z", "core"), ("x", "y"))
    return jax.shard_map(local, mesh=torus, in_specs=in_specs, out_specs=out_specs, check_vma=False)
```

```python
import functools

import jax
import jax.numpy as jnp
from jax import lax
from jax.experimental import pallas as pl
from jax.experimental.pallas import tpu as pltpu
from jax.sharding import Mesh
from jax.sharding import PartitionSpec as P

BLOCK = 128
SLAB = 1024
WIDE = 2048
LANES = 128
QUARTER = SLAB // 4
PIECE = SLAB // 16
AXES = ("x", "y", "z", "core")
F32, BF16, I16, I32 = jnp.float32, jnp.bfloat16, jnp.int16, jnp.int32

SENT = ((1, 0, 0, 1), (3, 2, 1, 0), (2, 3, 3, 2))
SECOND, CORE, OWNER, HALF, BASE = range(4, 9)


def shape(rows, columns, dtype):
    return jax.ShapeDtypeStruct((rows, columns), dtype)


def call(kernel, out, s, *args, flops=1 << 22, scratch=()):
    in_vmem = pl.BlockSpec(memory_space=pltpu.VMEM)
    return pl.pallas_call(
        kernel,
        out_shape=out,
        in_specs=[pl.BlockSpec(memory_space=pltpu.SMEM)] * len(s) + [in_vmem] * len(args),
        out_specs=jax.tree.map(lambda _: in_vmem, out),
        scratch_shapes=list(scratch),
        compiler_params=pltpu.CompilerParams(vmem_limit_bytes=16 << 20),
        cost_estimate=pl.CostEstimate(flops=flops, bytes_accessed=4 << 20, transcendentals=0),
    )(*s, *args)


def encode(v):
    top = jnp.max(jnp.abs(v), axis=1, keepdims=True)
    e = jnp.clip(jnp.floor(jnp.log2(top)) + 1.0, -100.0, 128.0)
    q = jnp.clip(jnp.round(v * jnp.exp2(15.0 - e)), -32767.0, 32767.0)
    tail = jnp.broadcast_to(e, (v.shape[0], LANES))
    return q.astype(I32).astype(I16), tail.astype(I32).astype(I16)


def put(ref, v):
    q, tail = encode(v)
    width = v.shape[1]
    ref[:, :width] = q
    ref[:, width:] = tail


def take(ref, rows=slice(None)):
    width = ref.shape[1] - LANES
    e = ref[rows, width:].astype(I32).astype(F32)
    scale = jnp.exp2(e - 15.0)[:, :1]
    return ref[rows, :width].astype(I32).astype(F32) * scale


def at(i, size):
    return pl.ds(pl.multiple_of(i * size, size), size)


def masked_block(m, density, i, j):
    block = density[i * BLOCK : (i + 1) * BLOCK, j * BLOCK : (j + 1) * BLOCK]
    return jnp.where(m[i, j] != 0, block, jnp.zeros_like(block))


def column_kernel(s, m, hbm, top_a, low_a, top_b, low_b, density, whole, sem):
    copies = []
    for i in range(4):
        rows = slice(i * 256, (i + 1) * 256)
        copies.append(pltpu.make_async_copy(hbm.at[rows, :SLAB], density.at[rows], sem.at[i]))
        copies[i].start()
    for i in range(8):
        if i % 2 == 0:
            copies[i // 2].wait()
        for j in range(8):
            whole[i * BLOCK : (i + 1) * BLOCK, j * BLOCK : (j + 1) * BLOCK] = masked_block(m, density, i, j)
    for i, (top, low) in enumerate(((top_a, low_a), (top_b, low_b))):
        for j in range(2):
            columns = at((s[BASE] + 2 * i + j) % 4, QUARTER)
            to = slice(j * QUARTER, (j + 1) * QUARTER)
            top[:, to] = whole[:512, columns]
            low[:, to] = whole[512:, columns]


def mask_kernel(m, density, out):
    for i in range(8):
        for j in range(16):
            out[i * BLOCK : (i + 1) * BLOCK, j * BLOCK : (j + 1) * BLOCK] = masked_block(m, density, i, j)


def first_kernel(i, coded, s, *refs):
    *parts, masked, out, left, acc = refs
    for half, (own, other) in enumerate(zip(parts[::2], parts[1::2])):

        @pl.when(s[i] // 2 == half)
        def _(own=own, other=other):
            left[:512] = own[:, at(s[i] % 2, QUARTER)]
            left[512:] = other[:, at(s[i] % 2, QUARTER)]

    dims = (((0,), (0,)), ((), ()))
    to = acc if coded else out
    for n in range(4):
        columns = slice(n * 512, (n + 1) * 512)
        to[:, columns] = lax.dot_general(
            left[:512], masked[at(s[CORE], 512), columns], dims, preferred_element_type=F32
        ) + lax.dot_general(
            left[512:], masked[at(1 - s[CORE], 512), columns], dims, preferred_element_type=F32
        )
    if coded:
        put(out, acc[...])


def first_product(i, s, parts, masked, coded=True):
    out = shape(QUARTER, WIDE + LANES, I16) if coded else shape(QUARTER, WIDE, F32)
    return call(
        functools.partial(first_kernel, i, coded),
        out,
        [s],
        *parts,
        masked,
        flops=2 * QUARTER * SLAB * WIDE,
        scratch=[pltpu.VMEM((SLAB, QUARTER), BF16), pltpu.VMEM((QUARTER, WIDE), F32)],
    )


def spread_kernel(s, own, a, b, c, *outs):
    for d, out in enumerate(outs):
        rows = at((s[SECOND] + d) % 4, PIECE)
        v = own[rows, :] + take(a, rows) + take(b, rows) + take(c, rows)
        if d == 0:
            out[...] = v
        else:
            put(out, v)


def gather_kernel(own, a, b, c, out):
    put(out, own[...] + take(a) + take(b) + take(c))


def join_kernel(*refs):
    *parts, out = refs
    for i, part in enumerate(parts):
        out[i * PIECE : (i + 1) * PIECE] = part[...]


def second_kernel(s, coded, masked, mine, theirs, left):
    pieces = []
    for j in range(4):
        sub = (s[SECOND] + 4 - j) % 4
        start = ((sub // 2) ^ s[CORE]) * 128 + (sub % 2) * 64
        rows = pl.ds(pl.multiple_of(start, 64), PIECE)
        left[rows, :] = take(coded, slice(j * PIECE, (j + 1) * PIECE)).astype(BF16)
        pieces.append((j, start))
    for n in range(4):
        columns = slice(n * 256, (n + 1) * 256)
        t = -2.0 * lax.dot_general(
            left[...],
            masked[columns, :],
            (((1,), (1,)), ((), ())),
            preferred_element_type=F32,
        )
        mine[:, columns] = t[:128]
        theirs[:, columns] = t[128:]

    for half in range(2):

        @pl.when((s[OWNER] == 1) & (s[HALF] == half))
        def _(half=half):
            for j, start in pieces:
                v = take(coded, slice(j * PIECE, (j + 1) * PIECE))
                v = 3.0 * v[:, half * SLAB : (half + 1) * SLAB]

                @pl.when(start < 128)
                def _(v=v, start=start):
                    mine[pl.ds(pl.multiple_of(start, 64), PIECE), :] += v

                @pl.when(start >= 128)
                def _(v=v, start=start):
                    theirs[pl.ds(pl.multiple_of(start - 128, 64), PIECE), :] += v


def second_product(s, coded, masked):
    return call(
        second_kernel,
        [shape(128, SLAB, F32)] * 2,
        [s],
        coded,
        masked,
        flops=2 * QUARTER * SLAB * WIDE,
        scratch=[pltpu.VMEM((QUARTER, WIDE), BF16)],
    )


def pair_kernel(mine, came, out):
    put(out, mine[...] + came[...])


def finish_kernel(a, b, c, d, out):
    out[...] = take(a) + take(b) + take(c) + take(d)


def place(x, y, z, core):
    return ((x % 4 * 4 + y % 4) * 4 + z % 4) * 2 + core


DEVICES = [(x, y, z, c) for x in range(4) for y in range(4) for z in range(4) for c in range(2)]


def send(v, to):
    return lax.ppermute(v, AXES, [(place(*d), place(*to(*d))) for d in DEVICES])


def own_quarter(y, x, z, core):
    return (z - jnp.where(core == 0, y, x)) & 3


def along(v, shift):
    def to(x, y, z, core):
        d = shift(x if core else y, z)
        return (x, y + d, z, core) if core else (x + d, y, z, core)

    return send(v, to)


def across(v, d):
    return send(v, lambda x, y, z, core: (x + d, y, z, core) if core else (x, y + d, z, core))


def swap(v):
    return lax.ppermute(v, "core", [(0, 1), (1, 0)])


def spread_column(top, low, z, core):
    came = lax.ppermute(low, "core", [(0, 1), (1, 0)])
    half = jnp.where(core == 0, top, came)
    axes = ("z", "core")
    came = lax.ppermute(half, axes, [(0, 2), (1, 7)])
    half = jnp.where(z == 0, half, came)
    came = lax.ppermute(half, axes, [(0, 6), (1, 3), (2, 4), (7, 5)])
    late = (z == 2) | ((z == 3) & (core == 0)) | ((z == 1) & (core == 1))
    half = jnp.where(late, came, half)
    return half, swap(half)


def coordinates():
    x, y, z, core = (lax.axis_index(a) for a in AXES)
    row = x * 4 + y
    own = own_quarter(y, x, z, core)
    values = [sum((own == i).astype(I32) * b for i, b in enumerate(sent)) for sent in SENT]
    values += [own, jnp.where(core == 0, y, x), core]
    values += [(z * 2 + core == row >> 1).astype(I32), row & 1, (x + y) & 3]
    s = jnp.zeros((16,), I32)
    index = jnp.arange(16, dtype=I32)
    for i, v in enumerate(values):
        s = jnp.where(index == i, v, s)
    return s, z, core


def local(density, block_mask):
    s, z, core = coordinates()
    in_smem = pl.BlockSpec(memory_space=pltpu.SMEM)
    top_a, low_a, top_b, low_b = pl.pallas_call(
        column_kernel,
        out_shape=[shape(512, 512, BF16)] * 4,
        in_specs=[in_smem, in_smem, pl.BlockSpec(memory_space=pltpu.HBM)],
        out_specs=[pl.BlockSpec(memory_space=pltpu.VMEM)] * 4,
        scratch_shapes=[pltpu.VMEM((SLAB, SLAB), BF16)] * 2 + [pltpu.SemaphoreType.DMA((4,))],
        compiler_params=pltpu.CompilerParams(vmem_limit_bytes=16 << 20),
        name="column",
    )(s, block_mask, density)
    masked = call(mask_kernel, shape(SLAB, WIDE, BF16), [block_mask], density)
    near = spread_column(top_a, low_a, z, core)
    far = spread_column(top_b, low_b, z, core)

    came = []
    for i, parts in enumerate((near, near + far, near + far)):
        v = first_product(i, s, parts, masked)
        came.append(along(v, lambda second, z: SENT[i][(z - second) % 4] - (z - second)))
    mine = first_product(3, s, near + far, masked, False)
    wide, coded = shape(PIECE, WIDE, F32), shape(PIECE, WIDE + LANES, I16)
    mine, *parts = call(spread_kernel, [wide, coded, coded, coded], [s], mine, *came)
    came = [across(parts[d - 1], d) for d in (2, 1, 3)]
    v = call(gather_kernel, coded, [], mine, *came)

    parts = [across(v, d) for d in (1, 2, 3)]
    v = call(join_kernel, shape(QUARTER, WIDE + LANES, I16), [], v, *parts)
    turns = (3, 1, 2, 0)
    quarters = []
    for j in turns:
        quarters.append(along(v, lambda second, z: j - second))
    came = []
    for j, v in zip(turns, quarters):
        mine, theirs = second_product(s, v, masked)
        theirs = swap(theirs)
        v = call(pair_kernel, shape(128, SLAB + LANES, I16), [], mine, theirs)
        came.append(send(v, lambda x, y, z, core: (x, y, x + y + z - j, core)))
    return call(finish_kernel, shape(128, SLAB, F32), [], *came)


def solution(mesh):
    torus = Mesh(mesh.devices.reshape(4, 4, 4, 2), AXES)
    in_specs = (P(("x", "y"), ("z", "core")),) * 2
    out_specs = P(("z", "core"), ("x", "y"))
    return jax.shard_map(local, mesh=torus, in_specs=in_specs, out_specs=out_specs, check_vma=False)
```

```python
import functools

import jax
import jax.numpy as jnp
from jax import lax
from jax.experimental import pallas as pl
from jax.experimental.pallas import tpu as pltpu
from jax.sharding import Mesh
from jax.sharding import PartitionSpec as P

BLOCK = 128
SLAB = 1024
WIDE = 2048
LANES = 128
QUARTER = SLAB // 4
PIECE = SLAB // 16
AXES = ("x", "y", "z", "core")
F32, BF16, I16, I32 = jnp.float32, jnp.bfloat16, jnp.int16, jnp.int32

DEVICES = [(x, y, z, c) for x in range(4) for y in range(4) for z in range(4) for c in range(2)]


def turns(x, y):
    late = {(x + 2) % 4, (y + 2) % 4}
    return [q for q in range(4) if q not in late] + sorted(late)


def facts(x, y, z, core):
    first, second = (y, x) if core else (x, y)
    own = first + z
    quarters = [(own + d) % 4 for d in range(4)]
    chosen = [(first - q) % 4 for q in turns(x, y)]
    row = x * 4 + y
    source = 0 if z == 0 else 1 if z == 1 + 2 * core else 3 if z == 2 else 2
    own_square = int(z * 2 + core == row // 2)
    return [*quarters, *chosen, second, core, own_square, row % 2, source, 0, 0, 0]


QUARTERS, CHOSEN, SECOND, CORE, OWNER, HALF, SOURCE = 0, 4, 8, 9, 10, 11, 12


def shape(rows, columns, dtype):
    return jax.ShapeDtypeStruct((rows, columns), dtype)


def call(kernel, out, s, *args, flops=1 << 22, scratch=()):
    in_vmem = pl.BlockSpec(memory_space=pltpu.VMEM)
    return pl.pallas_call(
        kernel,
        out_shape=out,
        in_specs=[pl.BlockSpec(memory_space=pltpu.SMEM)] * len(s) + [in_vmem] * len(args),
        out_specs=jax.tree.map(lambda _: in_vmem, out),
        scratch_shapes=list(scratch),
        compiler_params=pltpu.CompilerParams(vmem_limit_bytes=16 << 20),
        cost_estimate=pl.CostEstimate(flops=flops, bytes_accessed=4 << 20, transcendentals=0),
    )(*s, *args)


def encode(v):
    top = jnp.max(jnp.abs(v), axis=1, keepdims=True)
    e = jnp.clip(jnp.floor(jnp.log2(top)) + 1.0, -100.0, 128.0)
    q = jnp.clip(jnp.round(v * jnp.exp2(15.0 - e)), -32767.0, 32767.0)
    tail = jnp.broadcast_to(e, (v.shape[0], LANES))
    return q.astype(I32).astype(I16), tail.astype(I32).astype(I16)


def put(ref, v):
    q, tail = encode(v)
    width = v.shape[1]
    ref[:, :width] = q
    ref[:, width:] = tail


def take(ref, rows=slice(None)):
    width = ref.shape[1] - LANES
    e = ref[rows, width:].astype(I32).astype(F32)
    scale = jnp.exp2(e - 15.0)[:, :1]
    return ref[rows, :width].astype(I32).astype(F32) * scale


def at(i, size):
    return pl.ds(pl.multiple_of(i * size, size), size)


def masked_block(m, density, i, j):
    block = density[i * BLOCK : (i + 1) * BLOCK, j * BLOCK : (j + 1) * BLOCK]
    return jnp.where(m[i, j] != 0, block, jnp.zeros_like(block))


def column_kernel(m, hbm, *refs):
    *outs, density, sem = refs
    copies = []
    for i in range(4):
        rows = slice(i * 256, (i + 1) * 256)
        copies.append(pltpu.make_async_copy(hbm.at[rows, :SLAB], density.at[rows], sem.at[i]))
        copies[i].start()
    for i in range(8):
        if i % 2 == 0:
            copies[i // 2].wait()
        rows = slice(i % 4 * BLOCK, (i % 4 + 1) * BLOCK)
        for j in range(8):
            out = outs[i // 4 + j // 4 * 2]
            out[rows, j % 4 * BLOCK : (j % 4 + 1) * BLOCK] = masked_block(m, density, i, j)


def mask_kernel(m, density, out):
    for i in range(8):
        for j in range(16):
            out[i * BLOCK : (i + 1) * BLOCK, j * BLOCK : (j + 1) * BLOCK] = masked_block(m, density, i, j)


def first_kernel(d, s, own_a, other_a, own_b, other_b, masked, *refs):
    *outs, left, acc = refs
    quarter = s[QUARTERS + d]
    for half, (own, other) in enumerate(((own_a, other_a), (own_b, other_b))):

        @pl.when(quarter // 2 == half)
        def _(own=own, other=other):
            left[:512] = own[:, at(quarter % 2, QUARTER)]
            left[512:] = other[:, at(quarter % 2, QUARTER)]

    dims = (((0,), (0,)), ((), ()))
    to = acc if d == 2 else outs[0]
    for n in range(4):
        columns = slice(n * 512, (n + 1) * 512)
        to[:, columns] = lax.dot_general(
            left[:512], masked[at(s[CORE], 512), columns], dims, preferred_element_type=F32
        ) + lax.dot_general(
            left[512:], masked[at(1 - s[CORE], 512), columns], dims, preferred_element_type=F32
        )
    if d == 2:
        put(outs[0], acc[:128])
        put(outs[1], acc[128:])


def first_product(d, s, parts, masked):
    out = [shape(128, WIDE + LANES, I16)] * 2 if d == 2 else shape(QUARTER, WIDE, F32)
    return call(
        functools.partial(first_kernel, d),
        out,
        [s],
        *parts,
        masked,
        flops=2 * QUARTER * SLAB * WIDE,
        scratch=[pltpu.VMEM((SLAB, QUARTER), BF16), pltpu.VMEM((QUARTER, WIDE), F32)],
    )


def push_kernel(start, mine, came, out):
    add = slice(start, start + 128)
    rest = slice(128 - start, 256 - start)
    put(out.at[add], mine[add, :] + take(came))
    put(out.at[rest], mine[rest, :])


def spread_kernel(s, own, a, b, *outs):
    for d, out in enumerate(outs):
        rows = at((s[SECOND] + d) % 4, PIECE)
        v = own[rows, :] + take(a, rows) + take(b, rows)
        if d == 0:
            out[...] = v
        else:
            put(out, v)


def gather_kernel(own, a, b, c, out):
    put(out, own[...] + take(a) + take(b) + take(c))


def join_kernel(*refs):
    *parts, out = refs
    for i, part in enumerate(parts):
        out[i * PIECE : (i + 1) * PIECE] = part[...]


def second_kernel(i, s, *refs):
    *quarters, masked, mine, theirs, left, triple = refs
    own, back, ahead, *far = quarters
    d = s[CHOSEN + i]
    starts = []
    for j in range(4):
        sub = (s[SECOND] + 4 - j) % 4
        starts.append(((sub // 2) ^ s[CORE]) * 128 + (sub % 2) * 64)

    def unpack(refs):
        for j, start in enumerate(starts):
            size = refs[0].shape[0]
            ref, first = refs[j * PIECE // size], j * PIECE % size
            v = take(ref, slice(first, first + PIECE))
            rows = pl.ds(pl.multiple_of(start, 64), PIECE)
            left[rows, :] = v.astype(BF16)
            for half in range(2):

                @pl.when((s[OWNER] == 1) & (s[HALF] == half))
                def _(v=v, rows=rows, half=half):
                    triple[rows, :] = 3.0 * v[:, half * SLAB : (half + 1) * SLAB]

    for shift, refs in ((0, [own]), (1, [back]), (3, [ahead]), (2, far)):
        if refs:
            pl.when(d == shift)(functools.partial(unpack, refs))
    for n in range(4):
        columns = slice(n * 256, (n + 1) * 256)
        t = -2.0 * lax.dot_general(
            left[...],
            masked[columns, :],
            (((1,), (1,)), ((), ())),
            preferred_element_type=F32,
        )
        mine[:, columns] = t[:128]
        theirs[:, columns] = t[128:]

    @pl.when(s[OWNER] == 1)
    def _():
        mine[...] += triple[:128]
        theirs[...] += triple[128:]


def second_product(i, s, quarters, masked):
    return call(
        functools.partial(second_kernel, i),
        [shape(128, SLAB, F32)] * 2,
        [s],
        *quarters,
        masked,
        flops=2 * QUARTER * SLAB * WIDE,
        scratch=[pltpu.VMEM((QUARTER, WIDE), BF16), pltpu.VMEM((QUARTER, SLAB), F32)],
    )


def pair_kernel(mine, came, out):
    put(out, mine[...] + came[...])


def finish_kernel(a, b, c, d, out):
    out[...] = take(a) + take(b) + take(c) + take(d)


def place(x, y, z, core):
    return ((x % 4 * 4 + y % 4) * 4 + z % 4) * 2 + core


def send(v, to):
    return lax.ppermute(v, AXES, [(place(*d), place(*to(*d))) for d in DEVICES])


def along(v, d):
    return send(v, lambda x, y, z, core: (x, y + d, z, core) if core else (x + d, y, z, core))


def across(v, d):
    return send(v, lambda x, y, z, core: (x + d, y, z, core) if core else (x, y + d, z, core))


def swap(v):
    return lax.ppermute(v, "core", [(0, 1), (1, 0)])


def pick_kernel(key, s, *refs):
    *parts, out = refs
    for i, part in enumerate(parts):

        @pl.when(s[key] == i)
        def _(part=part):
            out[...] = part[...]


def pick(key, s, *parts):
    out = shape(*parts[0].shape, parts[0].dtype)
    return call(functools.partial(pick_kernel, key), out, [s], *parts)


def spread_column(s, top, low):
    half = pick(CORE, s, top, lax.ppermute(low, "core", [(0, 1), (1, 0)]))
    axes = ("z", "core")
    one = lax.ppermute(half, axes, [(0, 2), (1, 7)])
    two = lax.ppermute(half, axes, [(0, 6), (1, 3)])
    three = lax.ppermute(one, axes, [(2, 4), (7, 5)])
    half = pick(SOURCE, s, half, one, two, three)
    return half, swap(half)


def local(density, block_mask):
    table = jnp.asarray([facts(*d) for d in DEVICES], I32)
    s = lax.dynamic_index_in_dim(table, lax.axis_index(AXES), 0, False)
    top_a, low_a, top_b, low_b = pl.pallas_call(
        column_kernel,
        out_shape=[shape(512, 512, BF16)] * 4,
        in_specs=[pl.BlockSpec(memory_space=pltpu.SMEM), pl.BlockSpec(memory_space=pltpu.HBM)],
        out_specs=[pl.BlockSpec(memory_space=pltpu.VMEM)] * 4,
        scratch_shapes=[pltpu.VMEM((SLAB, SLAB), BF16), pltpu.SemaphoreType.DMA((4,))],
        compiler_params=pltpu.CompilerParams(vmem_limit_bytes=60 << 20),
        name="column",
    )(block_mask, density)
    masked = call(mask_kernel, shape(SLAB, WIDE, BF16), [block_mask], density)
    parts = spread_column(s, top_a, low_a)
    parts += spread_column(s, top_b, low_b)

    wide = shape(QUARTER, WIDE + LANES, I16)
    top, low = first_product(2, s, parts, masked)
    top = along(top, 1)
    low = along(low, -1)
    ahead, back, mine = (first_product(d, s, parts, masked) for d in (1, 3, 0))
    ahead = call(functools.partial(push_kernel, 0), wide, [], ahead, top)
    ahead = along(ahead, 1)
    back = call(functools.partial(push_kernel, 128), wide, [], back, low)
    back = along(back, -1)
    coded = shape(PIECE, WIDE + LANES, I16)
    outs = [shape(PIECE, WIDE, F32), coded, coded, coded]
    mine, *pieces = call(spread_kernel, outs, [s], mine, ahead, back)
    came = [across(pieces[d - 1], d) for d in (2, 1, 3)]
    v = call(gather_kernel, coded, [], mine, *came)

    pieces = [across(v, d) for d in (1, 2, 3)]
    own = call(join_kernel, wide, [], v, *pieces)
    back, ahead = along(own, 1), along(own, -1)
    top = along(back[:128], 1)
    low = along(ahead[128:], -1)
    came = []
    for i in range(4):
        quarters = [own, back, ahead] + [top, low] * (i >= 2)
        mine, theirs = second_product(i, s, quarters, masked)
        theirs = swap(theirs)
        v = call(pair_kernel, shape(128, SLAB + LANES, I16), [], mine, theirs)
        came.append(send(v, lambda x, y, z, core: (x, y, z + turns(x, y)[i], core)))
    return call(finish_kernel, shape(128, SLAB, F32), [], *came)


def solution(mesh):
    torus = Mesh(mesh.devices.reshape(4, 4, 4, 2), AXES)
    in_specs = (P(("x", "y"), ("z", "core")),) * 2
    out_specs = P(("z", "core"), ("x", "y"))
    return jax.shard_map(local, mesh=torus, in_specs=in_specs, out_specs=out_specs, check_vma=False)
```

```python
import functools

import jax
import jax.numpy as jnp
from jax import lax
from jax.experimental import pallas as pl
from jax.experimental.pallas import tpu as pltpu
from jax.sharding import Mesh
from jax.sharding import PartitionSpec as P

BLOCK = 128
SLAB = 1024
WIDE = 2048
LANES = 128
QUARTER = SLAB // 4
PIECE = SLAB // 16
AXES = ("x", "y", "z", "core")
F32, BF16, I16, I32 = jnp.float32, jnp.bfloat16, jnp.int16, jnp.int32

DEVICES = [(x, y, z, c) for x in range(4) for y in range(4) for z in range(4) for c in range(2)]


def turns(x, y):
    late = {(x + 2) % 4, (y + 2) % 4}
    return [q for q in range(4) if q not in late] + sorted(late)


def facts(x, y, z, core):
    first, second = (y, x) if core else (x, y)
    own = first + z
    quarters = [(own + d) % 4 for d in range(4)]
    chosen = [(first - q) % 4 for q in turns(x, y)]
    row = x * 4 + y
    source = 0 if z == 0 else 1 if z == 1 + 2 * core else 3 if z == 2 else 2
    own_square = int(z * 2 + core == row // 2)
    where = [turns(x, y).index(q) for q in range(4)]
    return [*quarters, *chosen, *where, second, core, own_square, row % 2, source] + [0] * 15


QUARTERS, CHOSEN, WHERE, SECOND, CORE, OWNER, HALF, SOURCE = 0, 4, 8, 12, 13, 14, 15, 16


def shape(rows, columns, dtype):
    return jax.ShapeDtypeStruct((rows, columns), dtype)


def call(kernel, out, s, *args, flops=1 << 22, scratch=()):
    in_vmem = pl.BlockSpec(memory_space=pltpu.VMEM)
    return pl.pallas_call(
        kernel,
        out_shape=out,
        in_specs=[pl.BlockSpec(memory_space=pltpu.SMEM)] * len(s) + [in_vmem] * len(args),
        out_specs=jax.tree.map(lambda _: in_vmem, out),
        scratch_shapes=list(scratch),
        compiler_params=pltpu.CompilerParams(vmem_limit_bytes=16 << 20),
        cost_estimate=pl.CostEstimate(flops=flops, bytes_accessed=4 << 20, transcendentals=0),
    )(*s, *args)


def encode(v):
    top = jnp.max(jnp.abs(v), axis=1, keepdims=True)
    e = jnp.clip(jnp.floor(jnp.log2(top)) + 1.0, -100.0, 128.0)
    q = jnp.clip(jnp.round(v * jnp.exp2(15.0 - e)), -32767.0, 32767.0)
    tail = jnp.broadcast_to(e, (v.shape[0], LANES))
    return q.astype(I32).astype(I16), tail.astype(I32).astype(I16)


def put(ref, v):
    q, tail = encode(v)
    width = v.shape[1]
    ref[:, :width] = q
    ref[:, width:] = tail


def take(ref, rows=slice(None)):
    width = ref.shape[1] - LANES
    e = ref[rows, width:].astype(I32).astype(F32)
    scale = jnp.exp2(e - 15.0)[:, :1]
    return ref[rows, :width].astype(I32).astype(F32) * scale


def at(i, size):
    return pl.ds(pl.multiple_of(i * size, size), size)


def masked_block(m, density, i, j):
    block = density[i * BLOCK : (i + 1) * BLOCK, j * BLOCK : (j + 1) * BLOCK]
    return jnp.where(m[i, j] != 0, block, jnp.zeros_like(block))


def column_kernel(m, density, *outs):
    for i in range(8):
        rows = slice(i % 4 * BLOCK, (i % 4 + 1) * BLOCK)
        for j in range(8):
            out = outs[i // 4 + j // 4 * 2]
            out[rows, j % 4 * BLOCK : (j % 4 + 1) * BLOCK] = masked_block(m, density, i, j)


def mask_kernel(m, density, out):
    for i in range(8):
        for j in range(16):
            out[i * BLOCK : (i + 1) * BLOCK, j * BLOCK : (j + 1) * BLOCK] = masked_block(m, density, i, j)


def first_kernel(d, s, own_a, other_a, own_b, other_b, masked, *refs):
    *outs, left, acc = refs
    quarter = s[QUARTERS + d]
    for half, (own, other) in enumerate(((own_a, other_a), (own_b, other_b))):

        @pl.when(quarter // 2 == half)
        def _(own=own, other=other):
            left[:512] = own[:, at(quarter % 2, QUARTER)]
            left[512:] = other[:, at(quarter % 2, QUARTER)]

    dims = (((0,), (0,)), ((), ()))
    to = acc if d == 2 else outs[0]
    for n in range(4):
        columns = slice(n * 512, (n + 1) * 512)
        to[:, columns] = lax.dot_general(
            left[:512], masked[at(s[CORE], 512), columns], dims, preferred_element_type=F32
        ) + lax.dot_general(
            left[512:], masked[at(1 - s[CORE], 512), columns], dims, preferred_element_type=F32
        )
    if d == 2:
        put(outs[0], acc[:128])
        put(outs[1], acc[128:])


def first_product(d, s, parts, masked):
    out = [shape(128, WIDE + LANES, I16)] * 2 if d == 2 else shape(QUARTER, WIDE, F32)
    return call(
        functools.partial(first_kernel, d),
        out,
        [s],
        *parts,
        masked,
        flops=2 * QUARTER * SLAB * WIDE,
        scratch=[pltpu.VMEM((SLAB, QUARTER), BF16), pltpu.VMEM((QUARTER, WIDE), F32)],
    )


def push_kernel(start, mine, came, out):
    add = slice(start, start + 128)
    rest = slice(128 - start, 256 - start)
    put(out.at[add], mine[add, :] + take(came))
    put(out.at[rest], mine[rest, :])


def spread_kernel(s, own, a, b, *outs):
    for d, out in enumerate(outs):
        rows = at((s[SECOND] + d) % 4, PIECE)
        v = own[rows, :] + take(a, rows) + take(b, rows)
        if d == 0:
            out[...] = v
        else:
            put(out, v)


def gather_kernel(own, a, b, c, out):
    put(out, own[...] + take(a) + take(b) + take(c))


def join_kernel(*refs):
    *parts, out = refs
    for i, part in enumerate(parts):
        out[i * PIECE : (i + 1) * PIECE] = part[...]


def second_kernel(turn, s, *refs):
    *quarters, masked, mine, theirs, left, triple = refs
    own, back, ahead, *far = quarters
    starts = []
    for j in range(4):
        sub = (s[SECOND] + 4 - j) % 4
        starts.append(((sub // 2) ^ s[CORE]) * 256 + (sub % 2) * 64)

    def unpack(i, refs):
        for j, start in enumerate(starts):
            size = refs[0].shape[0]
            ref, first = refs[j * PIECE // size], j * PIECE % size
            v = take(ref, slice(first, first + PIECE))
            rows = pl.ds(pl.multiple_of(start + i * 128, 64), PIECE)
            left[rows, :] = v.astype(BF16)
            for half in range(2):

                @pl.when((s[OWNER] == 1) & (s[HALF] == half))
                def _(v=v, rows=rows, half=half):
                    triple[rows, :] = 3.0 * v[:, half * SLAB : (half + 1) * SLAB]

    for i in range(2):
        for shift, refs in ((0, [own]), (1, [back]), (3, [ahead]), (2, far)):
            if refs:
                pl.when(s[CHOSEN + turn + i] == shift)(functools.partial(unpack, i, refs))

    for n in range(4):
        columns = slice(n * 256, (n + 1) * 256)
        t = -2.0 * lax.dot_general(
            left[...],
            masked[columns, :],
            (((1,), (1,)), ((), ())),
            preferred_element_type=F32,
        )
        mine[:, columns] = t[:256]
        theirs[:, columns] = t[256:]

    @pl.when(s[OWNER] == 1)
    def _():
        mine[...] += triple[:256]
        theirs[...] += triple[256:]


def second_product(turn, s, quarters, masked):
    return call(
        functools.partial(second_kernel, turn),
        [shape(256, SLAB, F32)] * 2,
        [s],
        *quarters,
        masked,
        flops=4 * QUARTER * SLAB * WIDE,
        scratch=[pltpu.VMEM((512, WIDE), BF16), pltpu.VMEM((512, SLAB), F32)],
    )


def deal_kernel(s, mine_a, came_a, mine_b, came_b, *outs):
    for q, out in enumerate(outs):
        for i, (mine, came) in enumerate(((mine_a, came_a), (mine_b, came_b))):

            @pl.when(s[WHERE + q] // 2 == i)
            def _(q=q, out=out, mine=mine, came=came):
                rows = at(s[WHERE + q] % 2, 128)
                v = mine[rows, :] + came[rows, :]
                if q == 0:
                    out[...] = v
                else:
                    put(out, v)


def finish_kernel(own, a, b, c, out):
    out[...] = own[...] + take(a) + take(b) + take(c)


def place(x, y, z, core):
    return ((x % 4 * 4 + y % 4) * 4 + z % 4) * 2 + core


def send(v, to):
    return lax.ppermute(v, AXES, [(place(*d), place(*to(*d))) for d in DEVICES])


def along(v, d):
    return send(v, lambda x, y, z, core: (x, y + d, z, core) if core else (x + d, y, z, core))


def across(v, d):
    return send(v, lambda x, y, z, core: (x + d, y, z, core) if core else (x, y + d, z, core))


def swap(v):
    return lax.ppermute(v, "core", [(0, 1), (1, 0)])


def pick_kernel(key, s, *refs):
    *parts, out = refs
    for i, part in enumerate(parts):

        @pl.when(s[key] == i)
        def _(part=part):
            out[...] = part[...]


def pick(key, s, *parts):
    out = shape(*parts[0].shape, parts[0].dtype)
    return call(functools.partial(pick_kernel, key), out, [s], *parts)


def spread_column(s, top, low):
    half = pick(CORE, s, top, lax.ppermute(low, "core", [(0, 1), (1, 0)]))
    axes = ("z", "core")
    one = lax.ppermute(half, axes, [(0, 2), (1, 7)])
    two = lax.ppermute(half, axes, [(0, 6), (1, 3)])
    three = lax.ppermute(one, axes, [(2, 4), (7, 5)])
    half = pick(SOURCE, s, half, one, two, three)
    return half, swap(half)


def local(density, block_mask):
    table = jnp.asarray([facts(*d) for d in DEVICES], I32)
    s = lax.dynamic_index_in_dim(table, lax.axis_index(AXES), 0, False)
    outs = [shape(512, 512, BF16)] * 4
    top_a, low_a, top_b, low_b = call(column_kernel, outs, [block_mask], density[:, :SLAB])
    masked = call(mask_kernel, shape(SLAB, WIDE, BF16), [block_mask], density)
    parts = spread_column(s, top_a, low_a)
    parts += spread_column(s, top_b, low_b)

    wide = shape(QUARTER, WIDE + LANES, I16)
    top, low = first_product(2, s, parts, masked)
    top = along(top, 1)
    low = along(low, -1)
    ahead, back, mine = (first_product(d, s, parts, masked) for d in (1, 3, 0))
    ahead = call(functools.partial(push_kernel, 0), wide, [], ahead, top)
    ahead = along(ahead, 1)
    back = call(functools.partial(push_kernel, 128), wide, [], back, low)
    back = along(back, -1)
    coded = shape(PIECE, WIDE + LANES, I16)
    outs = [shape(PIECE, WIDE, F32), coded, coded, coded]
    mine, *pieces = call(spread_kernel, outs, [s], mine, ahead, back)
    came = [across(pieces[d - 1], d) for d in (2, 1, 3)]
    v = call(gather_kernel, coded, [], mine, *came)

    pieces = [across(v, d) for d in (1, 2, 3)]
    own = call(join_kernel, wide, [], v, *pieces)
    back, ahead = along(own, 1), along(own, -1)
    top = along(back[:128], 1)
    low = along(ahead[128:], -1)
    sums = []
    for i in (0, 2):
        quarters = [own, back, ahead] + [top, low] * (i == 2)
        mine, theirs = second_product(i, s, quarters, masked)
        sums += [mine, swap(theirs)]
    coded = shape(128, SLAB + LANES, I16)
    own, *parts = call(deal_kernel, [shape(128, SLAB, F32)] + [coded] * 3, [s], *sums)
    came = [send(parts[d - 1], lambda x, y, z, core: (x, y, z + d, core)) for d in (2, 1, 3)]
    return call(finish_kernel, shape(128, SLAB, F32), [], own, *came)


def solution(mesh):
    torus = Mesh(mesh.devices.reshape(4, 4, 4, 2), AXES)
    in_specs = (P(("x", "y"), ("z", "core")),) * 2
    out_specs = P(("z", "core"), ("x", "y"))
    return jax.shard_map(local, mesh=torus, in_specs=in_specs, out_specs=out_specs, check_vma=False)
```

```python
import functools

import jax
import jax.numpy as jnp
from jax import lax
from jax.experimental import pallas as pl
from jax.experimental.pallas import tpu as pltpu
from jax.sharding import Mesh
from jax.sharding import PartitionSpec as P

BLOCK = 128
SLAB = 1024
WIDE = 2048
LANES = 128
QUARTER = SLAB // 4
PIECE = SLAB // 16
AXES = ("x", "y", "z", "core")
F32, BF16, I16, I32 = jnp.float32, jnp.bfloat16, jnp.int16, jnp.int32

DEVICES = [(x, y, z, c) for x in range(4) for y in range(4) for z in range(4) for c in range(2)]


def turns(x, y):
    late = {(x + 2) % 4, (y + 2) % 4}
    return [q for q in range(4) if q not in late] + sorted(late)


def facts(x, y, z, core):
    first, second = (y, x) if core else (x, y)
    own = first + z
    quarters = [(own + d) % 4 for d in range(4)]
    chosen = [(first - q) % 4 for q in turns(x, y)]
    row = x * 4 + y
    source = 0 if z == 0 else 1 if z == 1 + 2 * core else 3 if z == 2 else 2
    own_square = int(z * 2 + core == row // 2)
    return [*quarters, *chosen, second, core, own_square, row % 2, source, 0, 0, 0]


QUARTERS, CHOSEN, SECOND, CORE, OWNER, HALF, SOURCE = 0, 4, 8, 9, 10, 11, 12


def shape(rows, columns, dtype):
    return jax.ShapeDtypeStruct((rows, columns), dtype)


def call(kernel, out, s, *args, flops=1 << 22, scratch=()):
    in_vmem = pl.BlockSpec(memory_space=pltpu.VMEM)
    return pl.pallas_call(
        kernel,
        out_shape=out,
        in_specs=[pl.BlockSpec(memory_space=pltpu.SMEM)] * len(s) + [in_vmem] * len(args),
        out_specs=jax.tree.map(lambda _: in_vmem, out),
        scratch_shapes=list(scratch),
        compiler_params=pltpu.CompilerParams(vmem_limit_bytes=16 << 20),
        cost_estimate=pl.CostEstimate(flops=flops, bytes_accessed=4 << 20, transcendentals=0),
    )(*s, *args)


def encode(v):
    top = jnp.max(jnp.abs(v), axis=1, keepdims=True)
    e = jnp.clip(jnp.floor(jnp.log2(top)) + 1.0, -100.0, 128.0)
    q = jnp.clip(jnp.round(v * jnp.exp2(15.0 - e)), -32767.0, 32767.0)
    tail = jnp.broadcast_to(e, (v.shape[0], LANES))
    return q.astype(I32).astype(I16), tail.astype(I32).astype(I16)


def put(ref, v):
    q, tail = encode(v)
    width = v.shape[1]
    ref[:, :width] = q
    ref[:, width:] = tail


def take(ref, rows=slice(None)):
    width = ref.shape[1] - LANES
    e = ref[rows, width:].astype(I32).astype(F32)
    scale = jnp.exp2(e - 15.0)[:, :1]
    return ref[rows, :width].astype(I32).astype(F32) * scale


def at(i, size):
    return pl.ds(pl.multiple_of(i * size, size), size)


def masked_block(m, density, i, j):
    block = density[i * BLOCK : (i + 1) * BLOCK, j * BLOCK : (j + 1) * BLOCK]
    return jnp.where(m[i, j] != 0, block, jnp.zeros_like(block))


def column_kernel(m, density, *outs):
    for i in range(8):
        rows = slice(i % 4 * BLOCK, (i % 4 + 1) * BLOCK)
        for j in range(8):
            out = outs[i // 4 + j // 4 * 2]
            out[rows, j % 4 * BLOCK : (j % 4 + 1) * BLOCK] = masked_block(m, density, i, j)


def mask_kernel(m, density, out):
    for i in range(8):
        for j in range(16):
            out[i * BLOCK : (i + 1) * BLOCK, j * BLOCK : (j + 1) * BLOCK] = masked_block(m, density, i, j)


def first_kernel(d, s, own_a, other_a, own_b, other_b, masked, *refs):
    *outs, left, acc = refs
    quarter = s[QUARTERS + d]
    for half, (own, other) in enumerate(((own_a, other_a), (own_b, other_b))):

        @pl.when(quarter // 2 == half)
        def _(own=own, other=other):
            left[:512] = own[:, at(quarter % 2, QUARTER)]
            left[512:] = other[:, at(quarter % 2, QUARTER)]

    dims = (((0,), (0,)), ((), ()))
    to = acc if d == 2 else outs[0]
    for n in range(4):
        columns = slice(n * 512, (n + 1) * 512)
        to[:, columns] = lax.dot_general(
            left[:512], masked[at(s[CORE], 512), columns], dims, preferred_element_type=F32
        ) + lax.dot_general(
            left[512:], masked[at(1 - s[CORE], 512), columns], dims, preferred_element_type=F32
        )
    if d == 2:
        put(outs[0], acc[:128])
        put(outs[1], acc[128:])


def first_product(d, s, parts, masked):
    out = [shape(128, WIDE + LANES, I16)] * 2 if d == 2 else shape(QUARTER, WIDE, F32)
    return call(
        functools.partial(first_kernel, d),
        out,
        [s],
        *parts,
        masked,
        flops=2 * QUARTER * SLAB * WIDE,
        scratch=[pltpu.VMEM((SLAB, QUARTER), BF16), pltpu.VMEM((QUARTER, WIDE), F32)],
    )


def push_kernel(start, mine, came, out):
    add = slice(start, start + 128)
    rest = slice(128 - start, 256 - start)
    put(out.at[add], mine[add, :] + take(came))
    put(out.at[rest], mine[rest, :])


def spread_kernel(s, own, a, b, *outs):
    for d, out in enumerate(outs):
        rows = at((s[SECOND] + d) % 4, PIECE)
        v = own[rows, :] + take(a, rows) + take(b, rows)
        if d == 0:
            out[...] = v
        else:
            put(out, v)


def gather_kernel(own, a, b, c, out):
    put(out, own[...] + take(a) + take(b) + take(c))


def join_kernel(*refs):
    *parts, out = refs
    for i, part in enumerate(parts):
        out[i * PIECE : (i + 1) * PIECE] = part[...]


def second_kernel(turn, s, *refs):
    *quarters, masked, mine, theirs, left, triple = refs
    own, back, ahead, *far = quarters
    starts = []
    for j in range(4):
        sub = (s[SECOND] + 4 - j) % 4
        starts.append(((sub // 2) ^ s[CORE]) * 256 + (sub % 2) * 64)

    def unpack(i, refs):
        for j, start in enumerate(starts):
            size = refs[0].shape[0]
            ref, first = refs[j * PIECE // size], j * PIECE % size
            v = take(ref, slice(first, first + PIECE))
            rows = pl.ds(pl.multiple_of(start + i * 128, 64), PIECE)
            left[rows, :] = v.astype(BF16)
            for half in range(2):

                @pl.when((s[OWNER] == 1) & (s[HALF] == half))
                def _(v=v, rows=rows, half=half):
                    triple[rows, :] = 3.0 * v[:, half * SLAB : (half + 1) * SLAB]

    for i in range(2):
        for shift, refs in ((0, [own]), (1, [back]), (3, [ahead]), (2, far)):
            if refs:
                pl.when(s[CHOSEN + turn + i] == shift)(functools.partial(unpack, i, refs))

    for n in range(4):
        columns = slice(n * 256, (n + 1) * 256)
        t = -2.0 * lax.dot_general(
            left[...],
            masked[columns, :],
            (((1,), (1,)), ((), ())),
            preferred_element_type=F32,
        )
        mine[:, columns] = t[:256]
        theirs[:, columns] = t[256:]

    @pl.when(s[OWNER] == 1)
    def _():
        mine[...] += triple[:256]
        theirs[...] += triple[256:]


def second_product(turn, s, quarters, masked):
    return call(
        functools.partial(second_kernel, turn),
        [shape(256, SLAB, F32)] * 2,
        [s],
        *quarters,
        masked,
        flops=4 * QUARTER * SLAB * WIDE,
        scratch=[pltpu.VMEM((512, WIDE), BF16), pltpu.VMEM((512, SLAB), F32)],
    )


def deal_kernel(mine, came, *outs):
    for i, out in enumerate(outs):
        rows = slice(i * 128, (i + 1) * 128)
        put(out, mine[rows, :] + came[rows, :])


def finish_kernel(a, b, c, d, out):
    out[...] = take(a) + take(b) + take(c) + take(d)


def place(x, y, z, core):
    return ((x % 4 * 4 + y % 4) * 4 + z % 4) * 2 + core


def send(v, to):
    return lax.ppermute(v, AXES, [(place(*d), place(*to(*d))) for d in DEVICES])


def along(v, d):
    return send(v, lambda x, y, z, core: (x, y + d, z, core) if core else (x + d, y, z, core))


def across(v, d):
    return send(v, lambda x, y, z, core: (x + d, y, z, core) if core else (x, y + d, z, core))


def swap(v):
    return lax.ppermute(v, "core", [(0, 1), (1, 0)])


def pick_kernel(key, s, *refs):
    *parts, out = refs
    for i, part in enumerate(parts):

        @pl.when(s[key] == i)
        def _(part=part):
            out[...] = part[...]


def pick(key, s, *parts):
    out = shape(*parts[0].shape, parts[0].dtype)
    return call(functools.partial(pick_kernel, key), out, [s], *parts)


def spread_column(s, top, low):
    half = pick(CORE, s, top, lax.ppermute(low, "core", [(0, 1), (1, 0)]))
    axes = ("z", "core")
    one = lax.ppermute(half, axes, [(0, 2), (1, 7)])
    two = lax.ppermute(half, axes, [(0, 6), (1, 3)])
    three = lax.ppermute(one, axes, [(2, 4), (7, 5)])
    half = pick(SOURCE, s, half, one, two, three)
    return half, swap(half)


def local(density, block_mask):
    table = jnp.asarray([facts(*d) for d in DEVICES], I32)
    s = lax.dynamic_index_in_dim(table, lax.axis_index(AXES), 0, False)
    outs = [shape(512, 512, BF16)] * 4
    top_a, low_a, top_b, low_b = call(column_kernel, outs, [block_mask], density[:, :SLAB])
    masked = call(mask_kernel, shape(SLAB, WIDE, BF16), [block_mask], density)
    parts = spread_column(s, top_a, low_a)
    parts += spread_column(s, top_b, low_b)

    wide = shape(QUARTER, WIDE + LANES, I16)
    top, low = first_product(2, s, parts, masked)
    top = along(top, 1)
    low = along(low, -1)
    ahead, back, mine = (first_product(d, s, parts, masked) for d in (1, 3, 0))
    ahead = call(functools.partial(push_kernel, 0), wide, [], ahead, top)
    ahead = along(ahead, 1)
    back = call(functools.partial(push_kernel, 128), wide, [], back, low)
    back = along(back, -1)
    coded = shape(PIECE, WIDE + LANES, I16)
    outs = [shape(PIECE, WIDE, F32), coded, coded, coded]
    mine, *pieces = call(spread_kernel, outs, [s], mine, ahead, back)
    came = [across(pieces[d - 1], d) for d in (2, 1, 3)]
    v = call(gather_kernel, coded, [], mine, *came)

    pieces = [across(v, d) for d in (1, 2, 3)]
    own = call(join_kernel, wide, [], v, *pieces)
    back, ahead = along(own, 1), along(own, -1)
    top = along(back[:128], 1)
    low = along(ahead[128:], -1)
    came = []
    for i in (0, 2):
        quarters = [own, back, ahead] + [top, low] * (i == 2)
        mine, theirs = second_product(i, s, quarters, masked)
        theirs = swap(theirs)
        outs = [shape(128, SLAB + LANES, I16)] * 2
        parts = call(deal_kernel, outs, [], mine, theirs)
        for j, v in enumerate(parts):
            came.append(send(v, lambda x, y, z, core: (x, y, z + turns(x, y)[i + j], core)))
    return call(finish_kernel, shape(128, SLAB, F32), [], *came)


def solution(mesh):
    torus = Mesh(mesh.devices.reshape(4, 4, 4, 2), AXES)
    in_specs = (P(("x", "y"), ("z", "core")),) * 2
    out_specs = P(("z", "core"), ("x", "y"))
    return jax.shard_map(local, mesh=torus, in_specs=in_specs, out_specs=out_specs, check_vma=False)
```

```python
import functools

import jax
import jax.numpy as jnp
from jax import lax
from jax.experimental import pallas as pl
from jax.experimental.pallas import tpu as pltpu
from jax.sharding import Mesh
from jax.sharding import PartitionSpec as P

BLOCK = 128
SLAB = 1024
WIDE = 2048
LANES = 128
QUARTER = SLAB // 4
PIECE = SLAB // 16
AXES = ("x", "y", "z", "core")
F32, BF16, I16, I32 = jnp.float32, jnp.bfloat16, jnp.int16, jnp.int32

DEVICES = [(x, y, z, c) for x in range(4) for y in range(4) for z in range(4) for c in range(2)]


def turns(x, y):
    late = {(x + 2) % 4, (y + 2) % 4}
    return [q for q in range(4) if q not in late] + sorted(late)


def facts(x, y, z, core):
    first, second = (y, x) if core else (x, y)
    own, odd = first + z, first % 2
    step = -1 if odd else 1
    quarters = [(own + d) % 4 for d in (0, step, 2, -step)]
    codes = {0: 0, -step % 4: 1, step % 4: 2, 2: 4 if odd else 3}
    chosen = [codes[(first - q) % 4] for q in turns(x, y)]
    subs = [second, second ^ 1, second ^ 2, second ^ 3]
    source = 0 if z == 0 else 1 if z == 1 + 2 * core else 3 if z == 2 else 2
    own_square = int(z * 2 + core == (x * 4 + y) // 2)
    return [*quarters, *chosen, *subs, core, own_square, y % 2, source, odd] + [0] * 15


QUARTERS, CHOSEN, SUBS, CORE, OWNER, HALF, SOURCE, ODD = 0, 4, 8, 12, 13, 14, 15, 16


def shape(rows, columns, dtype):
    return jax.ShapeDtypeStruct((rows, columns), dtype)


def call(kernel, out, s, *args, flops=1 << 22, scratch=()):
    in_vmem = pl.BlockSpec(memory_space=pltpu.VMEM)
    return pl.pallas_call(
        kernel,
        out_shape=out,
        in_specs=[pl.BlockSpec(memory_space=pltpu.SMEM)] * len(s) + [in_vmem] * len(args),
        out_specs=jax.tree.map(lambda _: in_vmem, out),
        scratch_shapes=list(scratch),
        compiler_params=pltpu.CompilerParams(vmem_limit_bytes=16 << 20),
        cost_estimate=pl.CostEstimate(flops=flops, bytes_accessed=4 << 20, transcendentals=0),
    )(*s, *args)


def encode(v):
    top = jnp.max(jnp.abs(v), axis=1, keepdims=True)
    e = jnp.clip(jnp.floor(jnp.log2(top)) + 1.0, -100.0, 128.0)
    q = jnp.clip(jnp.round(v * jnp.exp2(15.0 - e)), -32767.0, 32767.0)
    tail = jnp.broadcast_to(e, (v.shape[0], LANES))
    return q.astype(I32).astype(I16), tail.astype(I32).astype(I16)


def put(ref, v):
    q, tail = encode(v)
    width = v.shape[1]
    ref[:, :width] = q
    ref[:, width:] = tail


def take(ref, rows=slice(None)):
    width = ref.shape[1] - LANES
    e = ref[rows, width:].astype(I32).astype(F32)
    scale = jnp.exp2(e - 15.0)[:, :1]
    return ref[rows, :width].astype(I32).astype(F32) * scale


def at(i, size):
    return pl.ds(pl.multiple_of(i * size, size), size)


def masked_block(m, density, i, j):
    block = density[i * BLOCK : (i + 1) * BLOCK, j * BLOCK : (j + 1) * BLOCK]
    return jnp.where(m[i, j] != 0, block, jnp.zeros_like(block))


def column_kernel(m, density, *outs):
    for i in range(8):
        rows = slice(i % 4 * BLOCK, (i % 4 + 1) * BLOCK)
        for j in range(8):
            out = outs[i // 4 + j // 4 * 2]
            out[rows, j % 4 * BLOCK : (j % 4 + 1) * BLOCK] = masked_block(m, density, i, j)


def mask_kernel(m, density, out):
    for i in range(8):
        for j in range(16):
            out[i * BLOCK : (i + 1) * BLOCK, j * BLOCK : (j + 1) * BLOCK] = masked_block(m, density, i, j)


def first_kernel(d, s, own_a, other_a, own_b, other_b, masked, *refs):
    *outs, left, acc = refs
    quarter = s[QUARTERS + d]
    for half, (own, other) in enumerate(((own_a, other_a), (own_b, other_b))):

        @pl.when(quarter // 2 == half)
        def _(own=own, other=other):
            left[:512] = own[:, at(quarter % 2, QUARTER)]
            left[512:] = other[:, at(quarter % 2, QUARTER)]

    dims = (((0,), (0,)), ((), ()))
    to = acc if d == 2 else outs[0]
    for n in range(4):
        columns = slice(n * 512, (n + 1) * 512)
        to[:, columns] = lax.dot_general(
            left[:512], masked[at(s[CORE], 512), columns], dims, preferred_element_type=F32
        ) + lax.dot_general(
            left[512:], masked[at(1 - s[CORE], 512), columns], dims, preferred_element_type=F32
        )
    if d == 2:
        for i, out in enumerate(outs):
            put(out, acc[at(s[ODD] ^ i, 128), :])


def first_product(d, s, parts, masked):
    out = [shape(128, WIDE + LANES, I16)] * 2 if d == 2 else shape(QUARTER, WIDE, F32)
    return call(
        functools.partial(first_kernel, d),
        out,
        [s],
        *parts,
        masked,
        flops=2 * QUARTER * SLAB * WIDE,
        scratch=[pltpu.VMEM((SLAB, QUARTER), BF16), pltpu.VMEM((QUARTER, WIDE), F32)],
    )


def push_kernel(i, s, mine, came, out):
    add, rest = at(s[ODD] ^ i, 128), at(s[ODD] ^ i ^ 1, 128)
    put(out.at[add], mine[add, :] + take(came))
    put(out.at[rest], mine[rest, :])


def cut_kernel(i, s, v, out):
    out[...] = v[at(s[ODD] ^ i, 128), :]


def spread_kernel(s, own, a, b, *outs):
    for d, out in enumerate(outs):
        rows = at(s[SUBS + d], PIECE)
        v = own[rows, :] + take(a, rows) + take(b, rows)
        if d == 0:
            out[...] = v
        else:
            put(out, v)


def gather_kernel(own, a, b, c, out):
    put(out, own[...] + take(a) + take(b) + take(c))


def join_kernel(*refs):
    *parts, out = refs
    for i, part in enumerate(parts):
        out[i * PIECE : (i + 1) * PIECE] = part[...]


def second_kernel(turn, s, *refs):
    *quarters, masked, mine, theirs, left, triple = refs
    own, near, next_, *far = quarters
    starts = []
    for j in range(4):
        sub = s[SUBS + j]
        starts.append(((sub // 2) ^ s[CORE]) * 256 + (sub % 2) * 64)

    def unpack(i, refs):
        for j, start in enumerate(starts):
            size = refs[0].shape[0]
            ref, first = refs[j * PIECE // size], j * PIECE % size
            v = take(ref, slice(first, first + PIECE))
            rows = pl.ds(pl.multiple_of(start + i * 128, 64), PIECE)
            left[rows, :] = v.astype(BF16)
            for half in range(2):

                @pl.when((s[OWNER] == 1) & (s[HALF] == half))
                def _(v=v, rows=rows, half=half):
                    triple[rows, :] = 3.0 * v[:, half * SLAB : (half + 1) * SLAB]

    for i in range(2):
        for code, refs in enumerate(([own], [near], [next_], far[::-1], far)):
            if refs:
                pl.when(s[CHOSEN + turn + i] == code)(functools.partial(unpack, i, refs))

    for n in range(4):
        columns = slice(n * 256, (n + 1) * 256)
        t = -2.0 * lax.dot_general(
            left[...],
            masked[columns, :],
            (((1,), (1,)), ((), ())),
            preferred_element_type=F32,
        )
        mine[:, columns] = t[:256]
        theirs[:, columns] = t[256:]

    @pl.when(s[OWNER] == 1)
    def _():
        mine[...] += triple[:256]
        theirs[...] += triple[256:]


def second_product(turn, s, quarters, masked):
    return call(
        functools.partial(second_kernel, turn),
        [shape(256, SLAB, F32)] * 2,
        [s],
        *quarters,
        masked,
        flops=4 * QUARTER * SLAB * WIDE,
        scratch=[pltpu.VMEM((512, WIDE), BF16), pltpu.VMEM((512, SLAB), F32)],
    )


def deal_kernel(mine, came, *outs):
    for i, out in enumerate(outs):
        rows = slice(i * 128, (i + 1) * 128)
        put(out, mine[rows, :] + came[rows, :])


def finish_kernel(a, b, c, d, out):
    out[...] = take(a) + take(b) + take(c) + take(d)


def place(x, y, z, core):
    return ((x % 4 * 4 + y % 4) * 4 + z % 4) * 2 + core


def send(v, to):
    return lax.ppermute(v, AXES, [(place(*d), place(*to(*d))) for d in DEVICES])


def along(v, flip):
    return send(v, lambda x, y, z, core: (x, y ^ flip, z, core) if core else (x ^ flip, y, z, core))


def across(v, flip):
    return send(v, lambda x, y, z, core: (x ^ flip, y, z, core) if core else (x, y ^ flip, z, core))


def swap(v):
    return lax.ppermute(v, "core", [(0, 1), (1, 0)])


def pick_kernel(key, s, *refs):
    *parts, out = refs
    for i, part in enumerate(parts):

        @pl.when(s[key] == i)
        def _(part=part):
            out[...] = part[...]


def pick(key, s, *parts):
    out = shape(*parts[0].shape, parts[0].dtype)
    return call(functools.partial(pick_kernel, key), out, [s], *parts)


def spread_column(s, top, low):
    half = pick(CORE, s, top, lax.ppermute(low, "core", [(0, 1), (1, 0)]))
    axes = ("z", "core")
    one = lax.ppermute(half, axes, [(0, 2), (1, 7)])
    two = lax.ppermute(half, axes, [(0, 6), (1, 3)])
    three = lax.ppermute(one, axes, [(2, 4), (7, 5)])
    half = pick(SOURCE, s, half, one, two, three)
    return half, swap(half)


def local(density, block_mask):
    table = jnp.asarray([facts(*d) for d in DEVICES], I32)
    s = lax.dynamic_index_in_dim(table, lax.axis_index(AXES), 0, False)
    outs = [shape(512, 512, BF16)] * 4
    top_a, low_a, top_b, low_b = call(column_kernel, outs, [block_mask], density[:, :SLAB])
    masked = call(mask_kernel, shape(SLAB, WIDE, BF16), [block_mask], density)
    parts = spread_column(s, top_a, low_a)
    parts += spread_column(s, top_b, low_b)

    wide = shape(QUARTER, WIDE + LANES, I16)
    halves = first_product(2, s, parts, masked)
    far = along(halves[1], 3)
    near = along(halves[0], 1)
    first, last, mine = (first_product(d, s, parts, masked) for d in (1, 3, 0))
    first = call(functools.partial(push_kernel, 0), wide, [s], first, far)
    first = along(first, 1)
    last = call(functools.partial(push_kernel, 1), wide, [s], last, near)
    last = along(last, 3)
    coded = shape(PIECE, WIDE + LANES, I16)
    outs = [shape(PIECE, WIDE, F32), coded, coded, coded]
    mine, *pieces = call(spread_kernel, outs, [s], mine, first, last)
    came = []
    for flip in (1, 2, 3):
        came.append(across(pieces[flip - 1], flip))
    v = call(gather_kernel, coded, [], mine, *came)

    pieces = []
    for flip in (1, 2, 3):
        pieces.append(across(v, flip))
    own = call(join_kernel, wide, [], v, *pieces)
    near = along(own, 1)
    next_ = along(own, 3)
    half = shape(128, WIDE + LANES, I16)
    cut = [call(functools.partial(cut_kernel, i), half, [s], v) for i, v in enumerate((next_, near))]
    far = [along(cut[0], 1)]
    far += [along(cut[1], 3)]
    came = []
    for i in (0, 2):
        quarters = [own, near, next_] + far * (i == 2)
        mine, theirs = second_product(i, s, quarters, masked)
        theirs = swap(theirs)
        outs = [shape(128, SLAB + LANES, I16)] * 2
        parts = call(deal_kernel, outs, [], mine, theirs)
        for j, v in enumerate(parts):
            came.append(send(v, lambda x, y, z, core: (x, y, z + turns(x, y)[i + j], core)))
    return call(finish_kernel, shape(128, SLAB, F32), [], *came)


def solution(mesh):
    torus = Mesh(mesh.devices.reshape(4, 4, 4, 2), AXES)
    in_specs = (P(("x", "y"), ("z", "core")),) * 2
    out_specs = P(("z", "core"), ("x", "y"))
    return jax.shard_map(local, mesh=torus, in_specs=in_specs, out_specs=out_specs, check_vma=False)
```

```python
import functools

import jax
import jax.numpy as jnp
from jax import lax
from jax.experimental import pallas as pl
from jax.experimental.pallas import tpu as pltpu
from jax.sharding import Mesh
from jax.sharding import PartitionSpec as P

BLOCK = 128
SLAB = 1024
WIDE = 2048
LANES = 128
QUARTER = SLAB // 4
PIECE = SLAB // 16
AXES = ("x", "y", "z", "core")
F32, BF16, I16, I32 = jnp.float32, jnp.bfloat16, jnp.int16, jnp.int32

DEVICES = [(x, y, z, c) for x in range(4) for y in range(4) for z in range(4) for c in range(2)]


def turns(x, y):
    late = {(x + 2) % 4, (y + 2) % 4}
    return [q for q in range(4) if q not in late] + sorted(late)


def facts(x, y, z, core):
    first, second = (y, x) if core else (x, y)
    own, odd = first + z, first % 2
    step = -1 if odd else 1
    quarters = [(own + d) % 4 for d in (0, step, 2, -step)]
    codes = {0: 0, -step % 4: 1, step % 4: 2, 2: 4 if odd else 3}
    chosen = [codes[(first - q) % 4] for q in turns(x, y)]
    subs = [second, second ^ 1, second ^ 2, second ^ 3]
    source = 0 if z == 0 else 1 if z == 1 + 2 * core else 3 if z == 2 else 2
    own_square = int(z * 2 + core == (x * 4 + y) // 2)
    where = [turns(x, y).index(((z ^ flip) - z) % 4) for flip in range(4)]
    return [*quarters, *chosen, *subs, *where, core, own_square, y % 2, source, odd] + [0] * 11


QUARTERS, CHOSEN, SUBS, WHERE, CORE, OWNER, HALF, SOURCE, ODD = 0, 4, 8, 12, 16, 17, 18, 19, 20


def shape(rows, columns, dtype):
    return jax.ShapeDtypeStruct((rows, columns), dtype)


def call(kernel, out, s, *args, flops=1 << 22, scratch=()):
    in_vmem = pl.BlockSpec(memory_space=pltpu.VMEM)
    return pl.pallas_call(
        kernel,
        out_shape=out,
        in_specs=[pl.BlockSpec(memory_space=pltpu.SMEM)] * len(s) + [in_vmem] * len(args),
        out_specs=jax.tree.map(lambda _: in_vmem, out),
        scratch_shapes=list(scratch),
        compiler_params=pltpu.CompilerParams(vmem_limit_bytes=16 << 20),
        cost_estimate=pl.CostEstimate(flops=flops, bytes_accessed=4 << 20, transcendentals=0),
    )(*s, *args)


def encode(v):
    top = jnp.max(jnp.abs(v), axis=1, keepdims=True)
    e = jnp.clip(jnp.floor(jnp.log2(top)) + 1.0, -100.0, 128.0)
    q = jnp.clip(jnp.round(v * jnp.exp2(15.0 - e)), -32767.0, 32767.0)
    tail = jnp.broadcast_to(e, (v.shape[0], LANES))
    return q.astype(I32).astype(I16), tail.astype(I32).astype(I16)


def put(ref, v):
    q, tail = encode(v)
    width = v.shape[1]
    ref[:, :width] = q
    ref[:, width:] = tail


def take(ref, rows=slice(None)):
    width = ref.shape[1] - LANES
    e = ref[rows, width:].astype(I32).astype(F32)
    scale = jnp.exp2(e - 15.0)[:, :1]
    return ref[rows, :width].astype(I32).astype(F32) * scale


def at(i, size):
    return pl.ds(pl.multiple_of(i * size, size), size)


def masked_block(m, density, i, j):
    block = density[i * BLOCK : (i + 1) * BLOCK, j * BLOCK : (j + 1) * BLOCK]
    return jnp.where(m[i, j] != 0, block, jnp.zeros_like(block))


def column_kernel(m, density, *outs):
    for i in range(8):
        rows = slice(i % 4 * BLOCK, (i % 4 + 1) * BLOCK)
        for j in range(8):
            out = outs[i // 4 + j // 4 * 2]
            out[rows, j % 4 * BLOCK : (j % 4 + 1) * BLOCK] = masked_block(m, density, i, j)


def mask_kernel(m, density, out):
    for i in range(8):
        for j in range(16):
            out[i * BLOCK : (i + 1) * BLOCK, j * BLOCK : (j + 1) * BLOCK] = masked_block(m, density, i, j)


def first_kernel(d, s, own_a, other_a, own_b, other_b, masked, *refs):
    *outs, left, acc = refs
    quarter = s[QUARTERS + d]
    for half, (own, other) in enumerate(((own_a, other_a), (own_b, other_b))):

        @pl.when(quarter // 2 == half)
        def _(own=own, other=other):
            left[:512] = own[:, at(quarter % 2, QUARTER)]
            left[512:] = other[:, at(quarter % 2, QUARTER)]

    dims = (((0,), (0,)), ((), ()))
    to = acc if d == 2 else outs[0]
    for n in range(4):
        columns = slice(n * 512, (n + 1) * 512)
        to[:, columns] = lax.dot_general(
            left[:512], masked[at(s[CORE], 512), columns], dims, preferred_element_type=F32
        ) + lax.dot_general(
            left[512:], masked[at(1 - s[CORE], 512), columns], dims, preferred_element_type=F32
        )
    if d == 2:
        for i, out in enumerate(outs):
            put(out, acc[at(s[ODD] ^ i, 128), :])


def first_product(d, s, parts, masked):
    out = [shape(128, WIDE + LANES, I16)] * 2 if d == 2 else shape(QUARTER, WIDE, F32)
    return call(
        functools.partial(first_kernel, d),
        out,
        [s],
        *parts,
        masked,
        flops=2 * QUARTER * SLAB * WIDE,
        scratch=[pltpu.VMEM((SLAB, QUARTER), BF16), pltpu.VMEM((QUARTER, WIDE), F32)],
    )


def by_half(i, s, body):
    for odd in range(2):
        start = 128 * (odd ^ i)
        halves = slice(start, start + 128), slice(128 - start, 256 - start)
        pl.when(s[ODD] == odd)(functools.partial(body, *halves))


def push_kernel(i, s, mine, came, out):
    def body(add, rest):
        put(out.at[add], mine[add, :] + take(came))
        put(out.at[rest], mine[rest, :])

    by_half(i, s, body)


def cut_kernel(i, s, v, out):
    def body(half, _):
        out[...] = v[half, :]

    by_half(i, s, body)


def spread_kernel(s, own, a, b, *outs):
    for d, out in enumerate(outs):
        rows = at(s[SUBS + d], PIECE)
        v = own[rows, :] + take(a, rows) + take(b, rows)
        if d == 0:
            out[...] = v
        else:
            put(out, v)


def gather_kernel(own, a, b, c, out):
    put(out, own[...] + take(a) + take(b) + take(c))


def join_kernel(*refs):
    *parts, out = refs
    for i, part in enumerate(parts):
        out[i * PIECE : (i + 1) * PIECE] = part[...]


def second_kernel(turn, s, *refs):
    *quarters, masked, mine, theirs, left, triple = refs
    own, near, next_, *far = quarters
    starts = []
    for j in range(4):
        sub = s[SUBS + j]
        starts.append(((sub // 2) ^ s[CORE]) * 256 + (sub % 2) * 64)

    def unpack(i, refs):
        for j, start in enumerate(starts):
            size = refs[0].shape[0]
            ref, first = refs[j * PIECE // size], j * PIECE % size
            v = take(ref, slice(first, first + PIECE))
            rows = pl.ds(pl.multiple_of(start + i * 128, 64), PIECE)
            left[rows, :] = v.astype(BF16)
            for half in range(2):

                @pl.when((s[OWNER] == 1) & (s[HALF] == half))
                def _(v=v, rows=rows, half=half):
                    triple[rows, :] = 3.0 * v[:, half * SLAB : (half + 1) * SLAB]

    for i in range(2):
        for code, refs in enumerate(([own], [near], [next_], far[::-1], far)):
            if refs:
                pl.when(s[CHOSEN + turn + i] == code)(functools.partial(unpack, i, refs))

    for n in range(4):
        columns = slice(n * 256, (n + 1) * 256)
        t = -2.0 * lax.dot_general(
            left[...],
            masked[columns, :],
            (((1,), (1,)), ((), ())),
            preferred_element_type=F32,
        )
        mine[:, columns] = t[:256]
        theirs[:, columns] = t[256:]

    @pl.when(s[OWNER] == 1)
    def _():
        mine[...] += triple[:256]
        theirs[...] += triple[256:]


def second_product(turn, s, quarters, masked):
    return call(
        functools.partial(second_kernel, turn),
        [shape(256, SLAB, F32)] * 2,
        [s],
        *quarters,
        masked,
        flops=4 * QUARTER * SLAB * WIDE,
        scratch=[pltpu.VMEM((512, WIDE), BF16), pltpu.VMEM((512, SLAB), F32)],
    )


def deal_kernel(s, mine_a, came_a, mine_b, came_b, *outs):
    for q, out in enumerate(outs):
        for i, (mine, came) in enumerate(((mine_a, came_a), (mine_b, came_b))):

            @pl.when(s[WHERE + q] // 2 == i)
            def _(q=q, out=out, mine=mine, came=came):
                rows = at(s[WHERE + q] % 2, 128)
                v = mine[rows, :] + came[rows, :]
                if q == 0:
                    out[...] = v
                else:
                    put(out, v)


def finish_kernel(own, a, b, c, out):
    out[...] = own[...] + take(a) + take(b) + take(c)


def place(x, y, z, core):
    return ((x % 4 * 4 + y % 4) * 4 + z % 4) * 2 + core


def send(v, to):
    return lax.ppermute(v, AXES, [(place(*d), place(*to(*d))) for d in DEVICES])


def along(v, flip):
    return send(v, lambda x, y, z, core: (x, y ^ flip, z, core) if core else (x ^ flip, y, z, core))


def across(v, flip):
    return send(v, lambda x, y, z, core: (x ^ flip, y, z, core) if core else (x, y ^ flip, z, core))


def swap(v):
    return lax.ppermute(v, "core", [(0, 1), (1, 0)])


def pick_kernel(key, s, *refs):
    *parts, out = refs
    for i, part in enumerate(parts):

        @pl.when(s[key] == i)
        def _(part=part):
            out[...] = part[...]


def pick(key, s, *parts):
    out = shape(*parts[0].shape, parts[0].dtype)
    return call(functools.partial(pick_kernel, key), out, [s], *parts)


def spread_column(s, top, low):
    half = pick(CORE, s, top, lax.ppermute(low, "core", [(0, 1), (1, 0)]))
    axes = ("z", "core")
    one = lax.ppermute(half, axes, [(0, 2), (1, 7)])
    two = lax.ppermute(half, axes, [(0, 6), (1, 3)])
    three = lax.ppermute(one, axes, [(2, 4), (7, 5)])
    half = pick(SOURCE, s, half, one, two, three)
    return half, swap(half)


def local(density, block_mask):
    table = jnp.asarray([facts(*d) for d in DEVICES], I32)
    s = lax.dynamic_index_in_dim(table, lax.axis_index(AXES), 0, False)
    outs = [shape(512, 512, BF16)] * 4
    top_a, low_a, top_b, low_b = call(column_kernel, outs, [block_mask], density[:, :SLAB])
    masked = call(mask_kernel, shape(SLAB, WIDE, BF16), [block_mask], density)
    parts = spread_column(s, top_a, low_a)
    parts += spread_column(s, top_b, low_b)

    wide = shape(QUARTER, WIDE + LANES, I16)
    halves = first_product(2, s, parts, masked)
    far = along(halves[1], 3)
    near = along(halves[0], 1)
    first, last, mine = (first_product(d, s, parts, masked) for d in (1, 3, 0))
    first = call(functools.partial(push_kernel, 0), wide, [s], first, far)
    first = along(first, 1)
    last = call(functools.partial(push_kernel, 1), wide, [s], last, near)
    last = along(last, 3)
    coded = shape(PIECE, WIDE + LANES, I16)
    outs = [shape(PIECE, WIDE, F32), coded, coded, coded]
    mine, *pieces = call(spread_kernel, outs, [s], mine, first, last)
    came = []
    for flip in (1, 2, 3):
        came.append(across(pieces[flip - 1], flip))
    v = call(gather_kernel, coded, [], mine, *came)

    pieces = []
    for flip in (1, 2, 3):
        pieces.append(across(v, flip))
    own = call(join_kernel, wide, [], v, *pieces)
    near = along(own, 1)
    next_ = along(own, 3)
    half = shape(128, WIDE + LANES, I16)
    cut = [call(functools.partial(cut_kernel, i), half, [s], v) for i, v in enumerate((next_, near))]
    far = [along(cut[0], 1)]
    far += [along(cut[1], 3)]
    sums = []
    for i in (0, 2):
        quarters = [own, near, next_] + far * (i == 2)
        mine, theirs = second_product(i, s, quarters, masked)
        sums += [mine, swap(theirs)]
    coded = shape(128, SLAB + LANES, I16)
    own, *parts = call(deal_kernel, [shape(128, SLAB, F32)] + [coded] * 3, [s], *sums)
    came = []
    for flip in (1, 2, 3):
        came.append(send(parts[flip - 1], lambda x, y, z, core: (x, y, z ^ flip, core)))
    return call(finish_kernel, shape(128, SLAB, F32), [], own, *came)


def solution(mesh):
    torus = Mesh(mesh.devices.reshape(4, 4, 4, 2), AXES)
    in_specs = (P(("x", "y"), ("z", "core")),) * 2
    out_specs = P(("z", "core"), ("x", "y"))
    return jax.shard_map(local, mesh=torus, in_specs=in_specs, out_specs=out_specs, check_vma=False)
```

```python
import functools

import jax
import jax.numpy as jnp
from jax import lax
from jax.experimental import pallas as pl
from jax.experimental.pallas import tpu as pltpu
from jax.sharding import Mesh
from jax.sharding import PartitionSpec as P

BLOCK = 128
SLAB = 1024
WIDE = 2048
LANES = 128
QUARTER = SLAB // 4
PIECE = SLAB // 16
AXES = ("x", "y", "z", "core")
F32, BF16, I16, I32 = jnp.float32, jnp.bfloat16, jnp.int16, jnp.int32

DEVICES = [(x, y, z, c) for x in range(4) for y in range(4) for z in range(4) for c in range(2)]


def turns(x, y):
    late = {(x + 2) % 4, (y + 2) % 4}
    return [q for q in range(4) if q not in late] + sorted(late)


def facts(x, y, z, core):
    first, second = (y, x) if core else (x, y)
    own, odd = first + z, first % 2
    step = -1 if odd else 1
    quarters = [(own + d) % 4 for d in (0, step, 2, -step)]
    codes = {0: 0, -step % 4: 1, step % 4: 2, 2: 4 if odd else 3}
    chosen = [codes[(first - q) % 4] for q in turns(x, y)]
    subs = [second, second ^ 1, second ^ 2, second ^ 3]
    source = 0 if z == 0 else 1 if z == 1 + 2 * core else 3 if z == 2 else 2
    own_square = int(z * 2 + core == (x * 4 + y) // 2)
    where = [turns(x, y).index(q) for q in range(4)]
    return [*quarters, *chosen, *subs, *where, core, own_square, y % 2, source, odd] + [0] * 11


QUARTERS, CHOSEN, SUBS, WHERE, CORE, OWNER, HALF, SOURCE, ODD = 0, 4, 8, 12, 16, 17, 18, 19, 20


def shape(rows, columns, dtype):
    return jax.ShapeDtypeStruct((rows, columns), dtype)


def call(kernel, out, s, *args, flops=1 << 22, scratch=()):
    in_vmem = pl.BlockSpec(memory_space=pltpu.VMEM)
    return pl.pallas_call(
        kernel,
        out_shape=out,
        in_specs=[pl.BlockSpec(memory_space=pltpu.SMEM)] * len(s) + [in_vmem] * len(args),
        out_specs=jax.tree.map(lambda _: in_vmem, out),
        scratch_shapes=list(scratch),
        compiler_params=pltpu.CompilerParams(vmem_limit_bytes=16 << 20),
        cost_estimate=pl.CostEstimate(flops=flops, bytes_accessed=4 << 20, transcendentals=0),
    )(*s, *args)


def encode(v):
    top = jnp.max(jnp.abs(v), axis=1, keepdims=True)
    e = jnp.clip(jnp.floor(jnp.log2(top)) + 1.0, -100.0, 128.0)
    q = jnp.clip(jnp.round(v * jnp.exp2(15.0 - e)), -32767.0, 32767.0)
    tail = jnp.broadcast_to(e, (v.shape[0], LANES))
    return q.astype(I32).astype(I16), tail.astype(I32).astype(I16)


def put(ref, v):
    q, tail = encode(v)
    width = v.shape[1]
    ref[:, :width] = q
    ref[:, width:] = tail


def take(ref, rows=slice(None)):
    width = ref.shape[1] - LANES
    e = ref[rows, width:].astype(I32).astype(F32)
    scale = jnp.exp2(e - 15.0)[:, :1]
    return ref[rows, :width].astype(I32).astype(F32) * scale


def at(i, size):
    return pl.ds(pl.multiple_of(i * size, size), size)


def masked_block(m, density, i, j):
    block = density[i * BLOCK : (i + 1) * BLOCK, j * BLOCK : (j + 1) * BLOCK]
    return jnp.where(m[i, j] != 0, block, jnp.zeros_like(block))


def column_kernel(m, density, *outs):
    for i in range(8):
        rows = slice(i % 4 * BLOCK, (i % 4 + 1) * BLOCK)
        for j in range(8):
            out = outs[i // 4 + j // 4 * 2]
            out[rows, j % 4 * BLOCK : (j % 4 + 1) * BLOCK] = masked_block(m, density, i, j)


def mask_kernel(m, density, out):
    for i in range(8):
        for j in range(16):
            out[i * BLOCK : (i + 1) * BLOCK, j * BLOCK : (j + 1) * BLOCK] = masked_block(m, density, i, j)


def first_kernel(d, s, own_a, other_a, own_b, other_b, masked, *refs):
    *outs, left, acc = refs
    quarter = s[QUARTERS + d]
    for half, (own, other) in enumerate(((own_a, other_a), (own_b, other_b))):

        @pl.when(quarter // 2 == half)
        def _(own=own, other=other):
            left[:512] = own[:, at(quarter % 2, QUARTER)]
            left[512:] = other[:, at(quarter % 2, QUARTER)]

    dims = (((0,), (0,)), ((), ()))
    to = acc if d == 2 else outs[0]
    for n in range(4):
        columns = slice(n * 512, (n + 1) * 512)
        to[:, columns] = lax.dot_general(
            left[:512], masked[at(s[CORE], 512), columns], dims, preferred_element_type=F32
        ) + lax.dot_general(
            left[512:], masked[at(1 - s[CORE], 512), columns], dims, preferred_element_type=F32
        )
    if d == 2:
        for i, out in enumerate(outs):
            put(out, acc[at(s[ODD] ^ i, 128), :])


def first_product(d, s, parts, masked):
    out = [shape(128, WIDE + LANES, I16)] * 2 if d == 2 else shape(QUARTER, WIDE, F32)
    return call(
        functools.partial(first_kernel, d),
        out,
        [s],
        *parts,
        masked,
        flops=2 * QUARTER * SLAB * WIDE,
        scratch=[pltpu.VMEM((SLAB, QUARTER), BF16), pltpu.VMEM((QUARTER, WIDE), F32)],
    )


def by_half(i, s, body):
    for odd in range(2):
        start = 128 * (odd ^ i)
        halves = slice(start, start + 128), slice(128 - start, 256 - start)
        pl.when(s[ODD] == odd)(functools.partial(body, *halves))


def push_kernel(i, s, mine, came, out):
    def body(add, rest):
        put(out.at[add], mine[add, :] + take(came))
        put(out.at[rest], mine[rest, :])

    by_half(i, s, body)


def cut_kernel(i, s, v, out):
    def body(half, _):
        out[...] = v[half, :]

    by_half(i, s, body)


def spread_kernel(s, own, a, b, *outs):
    for d, out in enumerate(outs):
        rows = at(s[SUBS + d], PIECE)
        v = own[rows, :] + take(a, rows) + take(b, rows)
        if d == 0:
            out[...] = v
        else:
            put(out, v)


def gather_kernel(own, a, b, c, out):
    put(out, own[...] + take(a) + take(b) + take(c))


def join_kernel(*refs):
    *parts, out = refs
    for i, part in enumerate(parts):
        out[i * PIECE : (i + 1) * PIECE] = part[...]


def second_kernel(turn, s, *refs):
    *quarters, masked, mine, theirs, left, triple = refs
    own, near, next_, *far = quarters
    starts = []
    for j in range(4):
        sub = s[SUBS + j]
        starts.append(((sub // 2) ^ s[CORE]) * 256 + (sub % 2) * 64)

    def unpack(i, refs):
        for j, start in enumerate(starts):
            size = refs[0].shape[0]
            ref, first = refs[j * PIECE // size], j * PIECE % size
            v = take(ref, slice(first, first + PIECE))
            rows = pl.ds(pl.multiple_of(start + i * 128, 64), PIECE)
            left[rows, :] = v.astype(BF16)
            for half in range(2):

                @pl.when((s[OWNER] == 1) & (s[HALF] == half))
                def _(v=v, rows=rows, half=half):
                    triple[rows, :] = 3.0 * v[:, half * SLAB : (half + 1) * SLAB]

    for i in range(2):
        for code, refs in enumerate(([own], [near], [next_], far[::-1], far)):
            if refs:
                pl.when(s[CHOSEN + turn + i] == code)(functools.partial(unpack, i, refs))

    for n in range(4):
        columns = slice(n * 256, (n + 1) * 256)
        t = -2.0 * lax.dot_general(
            left[...],
            masked[columns, :],
            (((1,), (1,)), ((), ())),
            preferred_element_type=F32,
        )
        mine[:, columns] = t[:256]
        theirs[:, columns] = t[256:]

    @pl.when(s[OWNER] == 1)
    def _():
        mine[...] += triple[:256]
        theirs[...] += triple[256:]


def second_product(turn, s, quarters, masked):
    return call(
        functools.partial(second_kernel, turn),
        [shape(256, SLAB, F32)] * 2,
        [s],
        *quarters,
        masked,
        flops=4 * QUARTER * SLAB * WIDE,
        scratch=[pltpu.VMEM((512, WIDE), BF16), pltpu.VMEM((512, SLAB), F32)],
    )


def deal_kernel(s, mine_a, came_a, mine_b, came_b, *outs):
    for q, out in enumerate(outs):
        for i, (mine, came) in enumerate(((mine_a, came_a), (mine_b, came_b))):

            @pl.when(s[WHERE + q] // 2 == i)
            def _(q=q, out=out, mine=mine, came=came):
                rows = at(s[WHERE + q] % 2, 128)
                v = mine[rows, :] + came[rows, :]
                if q == 0:
                    out[...] = v
                else:
                    put(out, v)


def finish_kernel(own, a, b, c, out):
    out[...] = own[...] + take(a) + take(b) + take(c)


def place(x, y, z, core):
    return ((x % 4 * 4 + y % 4) * 4 + z % 4) * 2 + core


def send(v, to):
    return lax.ppermute(v, AXES, [(place(*d), place(*to(*d))) for d in DEVICES])


def along(v, flip):
    return send(v, lambda x, y, z, core: (x, y ^ flip, z, core) if core else (x ^ flip, y, z, core))


def across(v, flip):
    return send(v, lambda x, y, z, core: (x ^ flip, y, z, core) if core else (x, y ^ flip, z, core))


def swap(v):
    return lax.ppermute(v, "core", [(0, 1), (1, 0)])


def pick_kernel(key, s, *refs):
    *parts, out = refs
    for i, part in enumerate(parts):

        @pl.when(s[key] == i)
        def _(part=part):
            out[...] = part[...]


def pick(key, s, *parts):
    out = shape(*parts[0].shape, parts[0].dtype)
    return call(functools.partial(pick_kernel, key), out, [s], *parts)


def spread_column(s, top, low):
    half = pick(CORE, s, top, lax.ppermute(low, "core", [(0, 1), (1, 0)]))
    axes = ("z", "core")
    one = lax.ppermute(half, axes, [(0, 2), (1, 7)])
    two = lax.ppermute(half, axes, [(0, 6), (1, 3)])
    three = lax.ppermute(one, axes, [(2, 4), (7, 5)])
    half = pick(SOURCE, s, half, one, two, three)
    return half, swap(half)


def local(density, block_mask):
    table = jnp.asarray([facts(*d) for d in DEVICES], I32)
    s = lax.dynamic_index_in_dim(table, lax.axis_index(AXES), 0, False)
    outs = [shape(512, 512, BF16)] * 4
    top_a, low_a, top_b, low_b = call(column_kernel, outs, [block_mask], density[:, :SLAB])
    masked = call(mask_kernel, shape(SLAB, WIDE, BF16), [block_mask], density)
    parts = spread_column(s, top_a, low_a)
    parts += spread_column(s, top_b, low_b)

    wide = shape(QUARTER, WIDE + LANES, I16)
    halves = first_product(2, s, parts, masked)
    far = along(halves[1], 3)
    near = along(halves[0], 1)
    first, last, mine = (first_product(d, s, parts, masked) for d in (1, 3, 0))
    first = call(functools.partial(push_kernel, 0), wide, [s], first, far)
    first = along(first, 1)
    last = call(functools.partial(push_kernel, 1), wide, [s], last, near)
    last = along(last, 3)
    coded = shape(PIECE, WIDE + LANES, I16)
    outs = [shape(PIECE, WIDE, F32), coded, coded, coded]
    mine, *pieces = call(spread_kernel, outs, [s], mine, first, last)
    came = []
    for flip in (1, 2, 3):
        came.append(across(pieces[flip - 1], flip))
    v = call(gather_kernel, coded, [], mine, *came)

    pieces = []
    for flip in (1, 2, 3):
        pieces.append(across(v, flip))
    own = call(join_kernel, wide, [], v, *pieces)
    near = along(own, 1)
    next_ = along(own, 3)
    half = shape(128, WIDE + LANES, I16)
    cut = [call(functools.partial(cut_kernel, i), half, [s], v) for i, v in enumerate((next_, near))]
    far = [along(cut[0], 1)]
    far += [along(cut[1], 3)]
    sums = []
    for i in (0, 2):
        quarters = [own, near, next_] + far * (i == 2)
        mine, theirs = second_product(i, s, quarters, masked)
        sums += [mine, swap(theirs)]
    coded = shape(128, SLAB + LANES, I16)
    own, *parts = call(deal_kernel, [shape(128, SLAB, F32)] + [coded] * 3, [s], *sums)
    came = []
    for d in (1, 3, 2):
        came.append(send(parts[d - 1], lambda x, y, z, core: (x, y, z + d, core)))
    return call(finish_kernel, shape(128, SLAB, F32), [], own, *came)


def solution(mesh):
    torus = Mesh(mesh.devices.reshape(4, 4, 4, 2), AXES)
    in_specs = (P(("x", "y"), ("z", "core")),) * 2
    out_specs = P(("z", "core"), ("x", "y"))
    return jax.shard_map(local, mesh=torus, in_specs=in_specs, out_specs=out_specs, check_vma=False)
```
